768 devices in a mesh: seq: 16 (over y, core), head: 12 (over x, z_hi), rep: 4 (over z_lo).
Axes of the slice: x: 4, y: 8, z: 12 (z_hi: 3, z_lo: 4; z = z_hi * 4 + z_lo), core: 2. Of those that a mesh axis runs over, the one named last changes fastest.
Arguments:
- queries: bfloat16 [16384, 3072], P(('seq', 'rep'), 'head'), may hold values from -190 to 190
- keys: bfloat16 [16384, 3072], P(('seq', 'rep'), 'head'), may hold values from -6 to 6
- values: bfloat16 [16384, 3072], P(('seq', 'rep'), 'head'), may hold values from -6 to 6
- grad_output: bfloat16 [16384, 3072], P(('seq', 'rep'), 'head'), may hold values from -12 to 12
- out_weight: bfloat16 [3072, 3072], P('head'), may hold values from -0.109375 to 0.109375
- text_keys: bfloat16 [256, 3072], P(None, 'head'), may hold values from -7 to 7
- text_values: bfloat16 [256, 3072], P(None, 'head'), may hold values from -6 to 6
- mask_lists: int32 [128, 3], replicated, may hold values from 0 to 127, as said below
- text_owner: int32 [256], replicated, may hold values from 0 to 63, as said below
Outputs:
- query_grads: bfloat16 [16384, 3072], P(('seq', 'rep'), 'head')
- key_grads: bfloat16 [16384, 3072], P(('seq', 'rep'), 'head')
- value_grads: bfloat16 [16384, 3072], P(('seq', 'rep'), 'head')
- text_key_grads: bfloat16 [512, 3072], P(('seq', 'rep'), 'head')
- text_value_grads: bfloat16 [512, 3072], P(('seq', 'rep'), 'head')
The draws below stay inside these ranges and needn't reach their ends.
Inputs may be any that keep to these rules, and one draw needn't show every extreme that they name: Video tokens s * 256 to (s + 1) * 256 - 1 form slab s. Row t of mask_lists begins with t itself; its other 2 entries are distinct existing tiles other than t of the slabs t // 2 - 1, t // 2 and t // 2 + 1. `text_owner`: no slab owns more than 8 text tokens, and some slab owns exactly 8.
All inputs are finite; a program needn't handle non-finite values.
Results may differ from the reference program's by a relative error of at most 0.0156.
Values may be sent and summed in bfloat16 or wider, within the bound.
A program may use at most 32 MiB of HBM per device.

```python
import jax
import jax.numpy as jnp
from jax import lax

D = 3072
HEADS = 24
HD = 128
FRAME = 256
TILE = 128
KB = 3
TEXT = 256
FRAMES = 64
VIDEO = 16384
QTILES = 128
CAP = 8
SLOTS = 512
HH = 3072


def shared_floats(key):
    base = jax.random.fold_in(key, 5)
    key_q, key_t = jax.random.split(base, 2)
    queries = jnp.clip(jax.random.normal(key_q, (VIDEO, HEADS * HD), jnp.float32), -6.0, 6.0)
    text = jnp.clip(jax.random.normal(key_t, (TEXT, HEADS * HD), jnp.float32), -6.0, 6.0)
    return (queries, text)


def draw_queries(key, part):
    return shared_floats(key)[0].astype(jnp.bfloat16)


def draw_text_keys(key, part):
    return shared_floats(key)[1].astype(jnp.bfloat16)


def draw_mask_lists(key, part):
    per_slab = FRAME // TILE
    tiles = jnp.arange(QTILES, dtype=jnp.int32)
    first = (tiles // per_slab - 1) * per_slab
    offsets = jnp.arange(3 * per_slab, dtype=jnp.int32)
    candidates = first[:, None] + offsets[None, :]
    usable = (candidates >= 0) & (candidates < QTILES) & (candidates != tiles[:, None])
    random_part = jax.random.randint(jax.random.fold_in(key, 17), (QTILES, 3 * per_slab), 0, 1 << 20)
    ranking = jnp.where(usable, random_part * (3 * per_slab) + offsets[None, :], -1 - offsets[None, :])
    unused, picks = lax.top_k(ranking, KB - 1)
    chosen = jnp.take_along_axis(candidates, picks, axis=1)
    return jnp.concatenate([tiles[:, None], chosen], axis=1).astype(jnp.int32)


def draw_text_owner(key, part):
    key_f, key_o, key_s = jax.random.split(jax.random.fold_in(key, 11), 3)
    busiest = jax.random.randint(key_f, (), 0, FRAMES)
    placing = jax.random.permutation(key_o, TEXT)
    others = jax.random.permutation(key_s, (FRAMES - 1) * CAP)[:TEXT - CAP] // CAP
    others = (others + (others >= busiest).astype(jnp.int32)).astype(jnp.int32)
    assigned = jnp.concatenate([jnp.full((CAP,), busiest, jnp.int32), others])
    return jnp.zeros((TEXT,), jnp.int32).at[placing].set(assigned)


def steps_of(stream_key, shape, cuts, low, largest):
    level = 1.0
    for axis_at, shards_of in cuts:
        draws = jax.random.uniform(jax.random.fold_in(jax.random.fold_in(stream_key, 6), axis_at), (shards_of,), jnp.float32, low / len(cuts), largest / len(cuts))
        level = level * jnp.repeat(jnp.exp(draws), shape[axis_at] // shards_of).reshape((-1,) + (1,) * (len(shape) - 1 - axis_at))
    return level


def scatter_about(stream_key, dims, scale, most, pieces=(), held_as=jnp.bfloat16):
    values = scale * jax.random.normal(stream_key, dims, jnp.float32)
    if pieces:
        values = values * steps_of(stream_key, dims, pieces, -0.22, 0.18)
    return jnp.clip(values, -most, most).astype(held_as)


def setup_inputs(seed: int = 0) -> dict:
    arg_keys = jax.random.split(jax.random.key(seed), 10)
    return {
        "queries": draw_queries(jax.random.fold_in(arg_keys[9], 71), 0),
        "keys": scatter_about(arg_keys[1], (VIDEO, HH), 1.0, 6.0, ((0, 64), (1, 12))),
        "values": scatter_about(arg_keys[2], (VIDEO, HH), 1.0, 6.0, ((0, 64), (1, 12))),
        "grad_output": scatter_about(arg_keys[3], (VIDEO, D), 2.0, 12.0, ((0, 64), (1, 12))),
        "out_weight": scatter_about(arg_keys[4], (HH, D), D ** -0.5, 0.109375, ((0, 12),)),
        "text_keys": draw_text_keys(jax.random.fold_in(arg_keys[9], 71), 0),
        "text_values": scatter_about(arg_keys[6], (TEXT, HH), 1.0, 6.0, ((1, 12),)),
        "mask_lists": draw_mask_lists(jax.random.fold_in(arg_keys[9], 71), 0),
        "text_owner": draw_text_owner(jax.random.fold_in(arg_keys[9], 71), 0),
    }


def reference(queries, keys, values, grad_output, out_weight, text_keys, text_values, mask_lists, text_owner):
    scale = HD ** -0.5
    grad_heads = jnp.dot(grad_output, out_weight.T, preferred_element_type=jnp.float32).astype(jnp.bfloat16)
    q_all = queries.reshape(VIDEO, HEADS, HD)
    k_all = keys.reshape(VIDEO, HEADS, HD)
    v_all = values.reshape(VIDEO, HEADS, HD)
    g_all = grad_heads.reshape(VIDEO, HEADS, HD)
    text_k = text_keys.reshape(TEXT, HEADS, HD).astype(jnp.float32)
    text_v = text_values.reshape(TEXT, HEADS, HD).astype(jnp.float32)
    within = jnp.arange(TILE, dtype=jnp.int32)
    video_n = KB * TILE

    def step(carry, tile):
        key_acc, value_acc, tkey_acc, tvalue_acc = carry
        start = (tile * TILE).astype(jnp.int32)
        q_tile = lax.dynamic_slice_in_dim(q_all, start, TILE, 0).astype(jnp.float32)
        g_tile = lax.dynamic_slice_in_dim(g_all, start, TILE, 0).astype(jnp.float32)
        listed = lax.dynamic_index_in_dim(mask_lists, tile, 0, keepdims=False)
        index = (listed[:, None] * TILE + within[None, :]).reshape(-1).astype(jnp.int32)
        k_tile = jnp.concatenate([k_all[index].astype(jnp.float32), text_k], axis=0)
        v_tile = jnp.concatenate([v_all[index].astype(jnp.float32), text_v], axis=0)
        scores = scale * jnp.einsum("qhe,khe->hqk", q_tile, k_tile)
        top = jnp.max(scores, axis=2, keepdims=True)
        lse = top + jnp.log(jnp.sum(jnp.exp(scores - top), axis=2, keepdims=True))
        prob = jnp.exp(scores - lse)
        prob_half = lax.optimization_barrier(prob.astype(jnp.bfloat16)).astype(jnp.float32)
        attended = jnp.einsum("hqk,khe->qhe", prob_half, v_tile)
        delta = jnp.einsum("qhe,qhe->hq", g_tile, attended)[:, :, None]
        dprob = jnp.einsum("qhe,khe->hqk", g_tile, v_tile)
        dscore = lax.optimization_barrier((prob * (dprob - delta)).astype(jnp.bfloat16)).astype(jnp.float32)
        dq = (scale * jnp.einsum("hqk,khe->qhe", dscore, k_tile)).astype(jnp.bfloat16)
        dk = scale * jnp.einsum("hqk,qhe->khe", dscore, q_tile)
        dv = jnp.einsum("hqk,qhe->khe", prob_half, g_tile)
        key_acc = key_acc.at[index].add(dk[:video_n])
        value_acc = value_acc.at[index].add(dv[:video_n])
        tkey_acc = tkey_acc + dk[video_n:]
        tvalue_acc = tvalue_acc + dv[video_n:]
        return (key_acc, value_acc, tkey_acc, tvalue_acc), dq

    start_carry = (jnp.zeros((VIDEO, HEADS, HD), jnp.float32), jnp.zeros((VIDEO, HEADS, HD), jnp.float32),
                   jnp.zeros((TEXT, HEADS, HD), jnp.float32), jnp.zeros((TEXT, HEADS, HD), jnp.float32))
    carry, dq_tiles = lax.scan(step, start_carry, jnp.arange(QTILES, dtype=jnp.int32))
    key_acc, value_acc, tkey_acc, tvalue_acc = carry
    query_grads = dq_tiles.reshape(VIDEO, HEADS * HD)
    key_grads = key_acc.reshape(VIDEO, HEADS * HD).astype(jnp.bfloat16)
    value_grads = value_acc.reshape(VIDEO, HEADS * HD).astype(jnp.bfloat16)
    owner_hot = (text_owner[:, None] == jnp.arange(FRAMES, dtype=jnp.int32)[None, :]).astype(jnp.int32)
    rank = jnp.sum(owner_hot * (jnp.cumsum(owner_hot, axis=0) - 1), axis=1).astype(jnp.int32)
    slot = (text_owner * CAP + rank).astype(jnp.int32)
    text_key_grads = jnp.zeros((SLOTS, HEADS * HD), jnp.bfloat16).at[slot].set(
        tkey_acc.reshape(TEXT, HEADS * HD).astype(jnp.bfloat16))
    text_value_grads = jnp.zeros((SLOTS, HEADS * HD), jnp.bfloat16).at[slot].set(
        tvalue_acc.reshape(TEXT, HEADS * HD).astype(jnp.bfloat16))
    return (query_grads, key_grads, value_grads, text_key_grads, text_value_grads)
```

```python
import functools

import jax
import jax.numpy as jnp
from jax import lax
from jax.experimental import pallas as pl
from jax.experimental.pallas import tpu as pltpu
from jax.sharding import PartitionSpec as P

HD = 128
TILE = 128
CAP = 8
XS = 4
ZS = 3
NEG = -1e30
MESH = pl.DeviceIdType.MESH
F32 = jnp.float32
BF16 = jnp.bfloat16


def dot(a, b, contract):
    return lax.dot_general(a, b, (contract, ((), ())), preferred_element_type=F32)


def kernel(
    seqs,
    reps,
    mask_ref,
    owner_ref,
    q_hbm,
    k_hbm,
    v_hbm,
    g_hbm,
    w_hbm,
    tk_hbm,
    tv_hbm,
    dq_ref,
    dk_ref,
    dv_ref,
    tkg_ref,
    tvg_ref,
    q,
    kall,
    vall,
    gbuf,
    w,
    gacc,
    gh,
    kt,
    st,
    pt,
    dp,
    ds,
    hsend,
    hrecv,
    own,
    place,
    slots,
    trecv1,
    tsum,
    trecv2,
    t3,
    trecv3,
    local_sem,
    zs,
    zr,
    xss,
    xsr,
    xfs,
    xfr,
    hs,
    hr,
    t1s,
    t1r,
    t2s,
    t2r,
    t3s,
    t3r,
):
    seq = lax.axis_index("seq")
    head = lax.axis_index("head")
    rep = lax.axis_index("rep")
    ys = seqs // 2
    y, core = seq // 2, seq % 2
    x, z = head // ZS, head % ZS
    slab = seq * reps + rep
    heads = q.shape[1] // HD
    frame = q.shape[0]
    scale = HD ** (-0.5)

    def head_of(dx, dz):
        return ((x + dx + XS) % XS) * ZS + (z + dz + ZS) % ZS

    z_dev = [{"head": head_of(0, 1)}, {"head": head_of(0, -1)}]
    x_dev = [{"head": head_of(1, 0)}, {"head": head_of(-1, 0)}]
    nxt = (slab + 1) % (seqs * reps)
    prv = (slab + seqs * reps - 1) % (seqs * reps)
    s_dev = [
        {"seq": nxt // reps, "rep": nxt % reps},
        {"seq": prv // reps, "rep": prv % reps},
    ]
    core_dev = {"seq": y * 2 + 1 - core}
    y_dev = [{"seq": ((y + d) % ys) * 2 + core} for d in range(1, ys)]
    r_dev = [{"rep": (rep + d) % reps} for d in range(1, reps)]

    loads = [
        pltpu.make_async_copy(src, dst, local_sem.at[i])
        for i, (src, dst) in enumerate(
            [
                (q_hbm, q),
                (tk_hbm, kall.at[3]),
                (k_hbm, kall.at[1]),
                (g_hbm, gbuf.at[0, 0]),
                (w_hbm, w),
                (tv_hbm, vall.at[3]),
                (v_hbm, vall.at[1]),
            ]
        )
    ]
    for load in loads:
        load.start()

    barrier = pltpu.get_barrier_semaphore()
    partners = z_dev + x_dev + s_dev + [core_dev] + y_dev + r_dev
    for dev in partners:
        pl.semaphore_signal(barrier, inc=1, device_id=dev, device_id_type=MESH)
    pl.semaphore_wait(barrier, len(partners))

    def remote(src, dst, ssem, rsem, dev):
        return pltpu.make_async_remote_copy(
            src_ref=src, dst_ref=dst, send_sem=ssem, recv_sem=rsem, device_id=dev, device_id_type=MESH
        )

    def rows(c):
        return pl.ds(c * TILE, TILE)

    halves = frame // TILE

    zc = [
        [
            remote(g_hbm.at[rows(c)], gbuf.at[0, 1 + d, rows(c)], zs.at[d, c], zr.at[d, c], z_dev[d])
            for c in range(halves)
        ]
        for d in range(2)
    ]
    xc = {}
    xf = {}
    for b in range(3):
        for c in range(halves):
            for d in range(2):
                src = g_hbm.at[rows(c)] if b == 0 else gbuf.at[0, b, rows(c)]
                xc[b, c, d] = remote(
                    src, gbuf.at[1 + d, b, rows(c)], xss.at[d, b, c], xsr.at[d, b, c], x_dev[d]
                )
        for d in range(2):
            xf[b, d] = remote(
                gbuf.at[1 + d, b, rows(d)], gbuf.at[3, b, rows(d)], xfs.at[d, b], xfr.at[d, b], x_dev[d]
            )
    hk = [remote(k_hbm, kall.at[2 * d], hs.at[0, d], hr.at[0, d], s_dev[d]) for d in range(2)]
    hv = [remote(v_hbm, vall.at[2 * d], hs.at[1, d], hr.at[1, d], s_dev[d]) for d in range(2)]
    hg = [
        [
            remote(hsend.at[n, d], hrecv.at[n, d], hs.at[2 + n, d], hr.at[2 + n, d], s_dev[d])
            for d in range(2)
        ]
        for n in range(2)
    ]

    for c in range(halves):
        for d in range(2):
            zc[d][c].start()
    for c in range(halves):
        for d in range(2):
            xc[0, c, d].start()
    for d in range(2):
        hk[d].start()
    for d in range(2):
        hv[d].start()

    def hcols(h):
        return slice(h * HD, (h + 1) * HD)

    lane = lax.broadcasted_iota(jnp.int32, (1, frame), 1)
    tops = [None] * heads

    def scores(j):
        for h in range(heads):
            s = dot(kall[j, :, hcols(h)], q[:, hcols(h)], ((1,), (1,))) * scale
            for t in range(halves):
                part = s[t * TILE : (t + 1) * TILE]
                if j < 3:
                    tile = (slab - 1 + j) * halves + t
                    bias = jnp.zeros((1, frame), F32)
                    for c in range(halves):
                        hit = mask_ref[slab * halves + c, 0] == tile
                        for i in range(1, 3):
                            hit = hit | (mask_ref[slab * halves + c, i] == tile)
                        level = jnp.where(hit, jnp.float32(0.0), jnp.float32(NEG))
                        bias = jnp.where(lane // TILE == c, level, bias)
                    part = part + bias
                st[h, j * frame + t * TILE : j * frame + (t + 1) * TILE, :] = part
                top = jnp.max(part, axis=0, keepdims=True)
                tops[h] = top if tops[h] is None else jnp.maximum(tops[h], top)

    def transposed_keys(j):
        for h in range(heads):
            kt[h, :, j * frame : (j + 1) * frame] = kall[j, :, hcols(h)].T

    loads[0].wait()
    loads[1].wait()
    scores(3)
    loads[2].wait()
    scores(1)

    def forward(b):
        for d in range(2):
            xc[b, d, d].wait_recv()
            xf[b, d].start()

    def add_block(c, xslot, b):
        hd = head_of((0, -1, 1, 2)[xslot], (0, -1, 1)[b])
        cols = pl.ds(pl.multiple_of(hd * frame, frame), frame)
        gacc[rows(c), :] += dot(gbuf[xslot, b, rows(c), :], w[:, cols], ((1,), (1,)))

    forward(0)
    loads[3].wait()
    loads[4].wait()
    gacc[...] = jnp.zeros_like(gacc)
    for c in range(halves):
        add_block(c, 0, 0)

    owner = owner_ref[...]
    texts = owner.shape[1]
    row_i = lax.broadcasted_iota(jnp.int32, (texts, texts), 0)
    col_i = lax.broadcasted_iota(jnp.int32, (texts, texts), 1)
    owner_f = owner.astype(F32)
    owner_col = jnp.sum(jnp.where(row_i == col_i, owner_f, 0.0), axis=1, keepdims=True)
    same = (owner_col == owner_f) & (row_i < col_i)
    rank = jnp.sum(jnp.where(same, 1.0, 0.0), axis=0, keepdims=True).astype(jnp.int32)
    o_rep = owner % reps
    o_seq = owner // reps
    where_to = (((o_seq % 2) * ys + o_seq // 2) * reps + o_rep) * CAP + rank
    slot_i = lax.broadcasted_iota(jnp.int32, place.shape, 0)
    place[...] = jnp.where(slot_i == where_to, 1.0, 0.0).astype(BF16)
    transposed_keys(3)
    transposed_keys(1)

    for c in range(halves):
        for d in range(2):
            zc[d][c].wait_recv()
            for e in range(2):
                xc[1 + d, c, e].start()
        if c == 0:
            for d in range(2):
                xc[0, 1 - d, d].wait_recv()
            for e in range(1, 3):
                for cc in range(halves):
                    add_block(cc, e, 0)
    for b in range(1, 3):
        forward(b)
    for c in range(halves):
        xf[0, c].wait_recv()
        add_block(c, 3, 0)
        for b in range(1, 3):
            add_block(c, 0, b)
    for b in range(1, 3):
        for d in range(2):
            xc[b, 1 - d, d].wait_recv()
            for c in range(halves):
                add_block(c, 1 + d, b)
    for b in range(1, 3):
        for c in range(halves):
            xf[b, c].wait_recv()
            add_block(c, 3, b)
    gh[...] = gacc[...].astype(BF16)

    for d in range(2):
        hk[d].wait_recv()
        scores(2 * d)
    keys_all = st.shape[1]
    for h in range(heads):
        total = jnp.zeros((1, frame), F32)
        for r in range(0, keys_all, TILE):
            e = jnp.exp(st[h, r : r + TILE, :] - tops[h])
            total = total + jnp.sum(e, axis=0, keepdims=True)
            st[h, r : r + TILE, :] = e
        inv = 1.0 / total
        for r in range(0, keys_all, TILE):
            p = st[h, r : r + TILE, :] * inv
            st[h, r : r + TILE, :] = p
            pt[h, r : r + TILE, :] = p.astype(BF16)

    def value_part(j, h):
        return dot(pt[h, j * frame : (j + 1) * frame, :], gh[:, hcols(h)], ((1,), (0,)))

    def key_part(j, h):
        return dot(ds[h, j * frame : (j + 1) * frame, :], q[:, hcols(h)], ((1,), (0,))) * scale

    def text_first(n, part):
        for h in range(heads):
            placed = dot(place[...], part(3, h).astype(BF16), ((1,), (0,)))
            slots[n, :, hcols(h)] = placed.astype(BF16)
        half = slots.shape[1] // 2
        copy = remote(
            slots.at[n, pl.ds((1 - core) * half, half)], trecv1.at[n], t1s.at[n], t1r.at[n], core_dev
        )
        copy.start()
        return copy

    for d in range(2):
        for h in range(heads):
            hsend[0, d, :, hcols(h)] = value_part(2 - 2 * d, h).astype(BF16)
        hg[0][d].start()
    t1 = [None, None]
    t1[0] = text_first(0, value_part)
    for h in range(heads):
        own[0, :, hcols(h)] = value_part(1, h)

    loads[5].wait()
    loads[6].wait()
    delta = [jnp.zeros((1, frame), F32) for _ in range(heads)]

    def dprob(j):
        for h in range(heads):
            for t in range(halves):
                r = j * frame + t * TILE
                part = dot(vall[j, rows(t), hcols(h)], gh[:, hcols(h)], ((1,), (1,)))
                dp[h, r : r + TILE, :] = part
                delta[h] = delta[h] + jnp.sum(
                    pt[h, r : r + TILE, :].astype(F32) * part, axis=0, keepdims=True
                )

    dprob(3)
    dprob(1)

    block = reps * CAP

    def text_second(n):
        t1[n].wait_recv()
        half = trecv1.shape[1]
        mine = slots[n, pl.ds(core * half, half), :].astype(F32)
        tsum[n] = (mine + trecv1[n].astype(F32)).astype(BF16)
        copies = []
        for d in range(1, ys):
            copy = remote(
                tsum.at[n, pl.ds(((y + d) % ys) * block, block)],
                trecv2.at[n, d - 1],
                t2s.at[n, d - 1],
                t2r.at[n, d - 1],
                y_dev[d - 1],
            )
            copy.start()
            copies.append(copy)
        return copies

    def text_third(n, second):
        total = tsum[n, pl.ds(y * block, block), :].astype(F32)
        for d in range(1, ys):
            second[d - 1].wait_recv()
            total = total + trecv2[n, d - 1].astype(F32)
        t3[n] = total
        copies = []
        for d in range(1, reps):
            copy = remote(
                t3.at[n, pl.ds(((rep + d) % reps) * CAP, CAP)],
                trecv3.at[n, d - 1],
                t3s.at[n, d - 1],
                t3r.at[n, d - 1],
                r_dev[d - 1],
            )
            copy.start()
            copies.append(copy)
        return copies

    def text_last(n, third, out):
        total = t3[n, pl.ds(rep * CAP, CAP), :]
        for d in range(1, reps):
            third[d - 1].wait_recv()
            total = total + trecv3[n, d - 1]
        out[...] = total.astype(BF16)

    second = [None, None]
    third = [None, None]
    second[0] = text_second(0)
    for d in range(2):
        transposed_keys(2 * d)
    for d in range(2):
        hv[d].wait_recv()
        dprob(2 * d)

    def dscore(j):
        for h in range(heads):
            for t in range(halves):
                r = j * frame + t * TILE
                ds[h, r : r + TILE, :] = (
                    st[h, r : r + TILE, :] * (dp[h, r : r + TILE, :] - delta[h])
                ).astype(BF16)

    for d in range(2):
        dscore(2 - 2 * d)
        for h in range(heads):
            hsend[1, d, :, hcols(h)] = key_part(2 - 2 * d, h).astype(BF16)
        hg[1][d].start()
    dscore(3)
    t1[1] = text_first(1, key_part)
    dscore(1)
    second[1] = text_second(1)
    for h in range(heads):
        own[1, :, hcols(h)] = key_part(1, h)
    for h in range(heads):
        dqt = dot(kt[h], ds[h], ((1,), (0,))) * scale
        dq_ref[:, hcols(h)] = dqt.T.astype(BF16)
    third[0] = text_third(0, second[0])
    for d in range(2):
        hg[0][d].wait_recv()
    dv_ref[...] = (own[0] + hrecv[0, 0].astype(F32) + hrecv[0, 1].astype(F32)).astype(BF16)
    third[1] = text_third(1, second[1])
    for d in range(2):
        hg[1][d].wait_recv()
    dk_ref[...] = (own[1] + hrecv[1, 0].astype(F32) + hrecv[1, 1].astype(F32)).astype(BF16)
    text_last(0, third[0], tvg_ref)
    text_last(1, third[1], tkg_ref)

    sent = [copy for pair in zc for copy in pair] + list(xc.values()) + list(xf.values())
    sent += hk + hv + hg[0] + hg[1] + t1 + second[0] + second[1] + third[0] + third[1]
    for copy in sent:
        copy.wait_send()


def local(
    seqs,
    reps,
    queries,
    keys,
    values,
    grad_output,
    out_weight,
    text_keys,
    text_values,
    mask_lists,
    text_owner,
):
    frame, width = queries.shape
    texts = text_keys.shape[0]
    heads = width // HD
    ys = seqs // 2
    slots = seqs * reps * CAP
    halves = frame // TILE
    block = reps * CAP
    total = 3 * frame + texts
    grads = jax.ShapeDtypeStruct((frame, width), BF16)
    text_grads = jax.ShapeDtypeStruct((CAP, width), BF16)
    hbm = pl.BlockSpec(memory_space=pl.ANY)
    vmem = pl.BlockSpec(memory_space=pltpu.VMEM)
    dma = pltpu.SemaphoreType.DMA
    return pl.pallas_call(
        functools.partial(kernel, seqs, reps),
        out_shape=(grads, grads, grads, text_grads, text_grads),
        in_specs=[pl.BlockSpec(memory_space=pltpu.SMEM), vmem] + [hbm] * 7,
        out_specs=(vmem,) * 5,
        scratch_shapes=[
            pltpu.VMEM((frame, width), BF16),
            pltpu.VMEM((4, frame, width), BF16),
            pltpu.VMEM((4, frame, width), BF16),
            pltpu.VMEM((XS, ZS, frame, width), BF16),
            pltpu.VMEM(out_weight.shape, BF16),
            pltpu.VMEM((frame, width), F32),
            pltpu.VMEM((frame, width), BF16),
            pltpu.VMEM((heads, HD, total), BF16),
            pltpu.VMEM((heads, total, frame), F32),
            pltpu.VMEM((heads, total, frame), BF16),
            pltpu.VMEM((heads, total, frame), F32),
            pltpu.VMEM((heads, total, frame), BF16),
            pltpu.VMEM((2, 2, frame, width), BF16),
            pltpu.VMEM((2, 2, frame, width), BF16),
            pltpu.VMEM((2, frame, width), F32),
            pltpu.VMEM((slots, texts), BF16),
            pltpu.VMEM((2, slots, width), BF16),
            pltpu.VMEM((2, slots // 2, width), BF16),
            pltpu.VMEM((2, slots // 2, width), BF16),
            pltpu.VMEM((2, ys - 1, block, width), BF16),
            pltpu.VMEM((2, block, width), F32),
            pltpu.VMEM((2, reps - 1, CAP, width), F32),
            dma((7,)),
            dma((2, halves)),
            dma((2, halves)),
            dma((2, 3, halves)),
            dma((2, 3, halves)),
            dma((2, 3)),
            dma((2, 3)),
            dma((4, 2)),
            dma((4, 2)),
            dma((2,)),
            dma((2,)),
            dma((2, ys - 1)),
            dma((2, ys - 1)),
            dma((2, reps - 1)),
            dma((2, reps - 1)),
        ],
        compiler_params=pltpu.CompilerParams(collective_id=0, has_side_effects=True),
    )(
        mask_lists,
        text_owner.reshape(1, texts),
        queries,
        keys,
        values,
        grad_output,
        out_weight,
        text_keys,
        text_values,
    )


def solution(mesh):
    rows = P(("seq", "rep"), "head")
    return jax.shard_map(
        functools.partial(local, mesh.shape["seq"], mesh.shape["rep"]),
        mesh=mesh,
        in_specs=(
            rows,
            rows,
            rows,
            rows,
            P("head", None),
            P(None, "head"),
            P(None, "head"),
            P(),
            P(),
        ),
        out_specs=(rows,) * 5,
        check_vma=False,
    )
```

```python
import functools

import jax
import jax.numpy as jnp
from jax import lax
from jax.experimental import pallas as pl
from jax.experimental.pallas import tpu as pltpu
from jax.sharding import PartitionSpec as P

HD = 128
TILE = 128
CAP = 8
XS = 4
ZS = 3
NEG = -1e30
MESH = pl.DeviceIdType.MESH
F32 = jnp.float32
BF16 = jnp.bfloat16


def dot(a, b, contract):
    return lax.dot_general(a, b, (contract, ((), ())), preferred_element_type=F32)


def kernel(
    seqs,
    reps,
    mask_ref,
    owner_ref,
    q_hbm,
    k_hbm,
    v_hbm,
    g_hbm,
    w_hbm,
    tk_hbm,
    tv_hbm,
    dq_ref,
    dk_ref,
    dv_ref,
    tkg_ref,
    tvg_ref,
    qall,
    kall,
    vall,
    gall,
    gbuf,
    w,
    gacc,
    kt,
    st,
    pt,
    dp,
    ds,
    hp,
    hpt,
    own,
    stat,
    place,
    slots,
    trecv1,
    tsum,
    trecv2,
    t3,
    trecv3,
    ready,
    local_sem,
    zs,
    zr,
    xss,
    xsr,
    xfs,
    xfr,
    hs,
    hr,
    t1s,
    t1r,
    t2s,
    t2r,
    t3s,
    t3r,
):
    seq = lax.axis_index("seq")
    head = lax.axis_index("head")
    rep = lax.axis_index("rep")
    ys = seqs // 2
    y, core = seq // 2, seq % 2
    x, z = head // ZS, head % ZS
    slabs = seqs * reps
    slab = seq * reps + rep
    frame, width = q_hbm.shape
    heads = width // HD
    halves = frame // TILE
    scale = HD ** (-0.5)

    def head_of(dx, dz):
        return ((x + dx + XS) % XS) * ZS + (z + dz + ZS) % ZS

    z_dev = [{"head": head_of(0, 1)}, {"head": head_of(0, -1)}]
    z_of = [(z + 1) % ZS, (z + ZS - 1) % ZS]
    x_dev = [{"head": head_of(1, 0)}, {"head": head_of(-1, 0)}]
    nxt = (slab + 1) % slabs
    prv = (slab + slabs - 1) % slabs
    s_dev = [
        {"seq": nxt // reps, "rep": nxt % reps},
        {"seq": prv // reps, "rep": prv % reps},
    ]
    core_dev = {"seq": y * 2 + 1 - core}
    y_dev = [{"seq": ((y + d) % ys) * 2 + core} for d in range(1, ys)]
    r_dev = [{"rep": (rep + d) % reps} for d in range(1, reps)]

    loads = [
        pltpu.make_async_copy(src, dst, local_sem.at[i])
        for i, (src, dst) in enumerate(
            [
                (q_hbm, qall.at[1]),
                (tk_hbm, kall.at[3]),
                (k_hbm, kall.at[1]),
                (g_hbm, gbuf.at[0, 0]),
                (w_hbm, w),
                (tv_hbm, vall.at[3]),
                (v_hbm, vall.at[1]),
            ]
        )
    ]
    for load in loads:
        load.start()

    for n in range(2):
        stat[n, 1] = jnp.full(stat.shape[2:], NEG, F32)

    barrier = pltpu.get_barrier_semaphore()
    partners = x_dev + s_dev + [core_dev] + y_dev + r_dev
    for dev in partners:
        pl.semaphore_signal(barrier, inc=1, device_id=dev, device_id_type=MESH)
    pl.semaphore_wait(barrier, len(partners) + z)
    for d in range(2):

        @pl.when(z_of[d] > z)
        def _():
            pl.semaphore_signal(barrier, inc=1, device_id=z_dev[d], device_id_type=MESH)

        @pl.when(z_of[d] < z)
        def _():
            pl.semaphore_signal(ready.at[1 - d], inc=1, device_id=z_dev[d], device_id_type=MESH)

    sent = []

    def remote(src, dst, ssem, rsem, dev):
        copy = pltpu.make_async_remote_copy(
            src_ref=src, dst_ref=dst, send_sem=ssem, recv_sem=rsem, device_id=dev, device_id_type=MESH
        )
        sent.append(copy)
        return copy

    def rows(c):
        return pl.ds(c * TILE, TILE)

    def hcols(h):
        return slice(h * HD, (h + 1) * HD)

    zc = [
        [
            remote(g_hbm.at[rows(c)], gbuf.at[0, 1 + d, rows(c)], zs.at[d, c], zr.at[d, c], z_dev[d])
            for c in range(halves)
        ]
        for d in range(2)
    ]
    xc = {}
    xf = {}
    for b in range(3):
        for c in range(halves):
            for d in range(2):
                src = g_hbm.at[rows(c)] if b == 0 else gbuf.at[0, b, rows(c)]
                xc[b, c, d] = remote(
                    src, gbuf.at[1 + d, b, rows(c)], xss.at[d, b, c], xsr.at[d, b, c], x_dev[d]
                )
        for d in range(2):
            xf[b, d] = remote(
                gbuf.at[1 + d, b, rows(d)], gbuf.at[3, b, rows(d)], xfs.at[d, b], xfr.at[d, b], x_dev[d]
            )

    def halo(n, src, dst):
        return [remote(src, dst.at[2 * d], hs.at[n, d], hr.at[n, d], s_dev[d]) for d in range(2)]

    hk = halo(0, k_hbm, kall)
    hv = halo(1, v_hbm, vall)
    hq = halo(2, q_hbm, qall)
    hg = halo(3, gall.at[1], gall)
    ha = halo(4, stat.at[0, 1], stat.at[0])
    hd = halo(5, stat.at[1, 1], stat.at[1])

    def z_send(d):
        for c in range(halves):
            zc[d][c].start()

    def z_send_later(d):
        pl.semaphore_wait(ready.at[d], 1)
        z_send(d)

    for d in range(2):

        @pl.when(z_of[d] < z)
        def _():
            z_send(d)

    for c in range(halves):
        for d in range(2):
            xc[0, c, d].start()
    for copy in hk + hv:
        copy.start()

    lane = lax.broadcasted_iota(jnp.int32, (1, frame), 1)

    def bias_of(tile, of_slab):
        bias = jnp.zeros((1, frame), F32)
        for c in range(halves):
            hit = mask_ref[0, of_slab * halves + c] == tile
            for i in range(1, 3):
                hit = hit | (mask_ref[i, of_slab * halves + c] == tile)
            level = jnp.where(hit, jnp.float32(0.0), jnp.float32(NEG))
            bias = jnp.where(lane // TILE == c, level, bias)
        return bias

    def scores(j):
        for h in range(heads):
            s = dot(kall[j, :, hcols(h)], qall[1, :, hcols(h)], ((1,), (1,))) * scale
            top = stat[0, 1, h : h + 1, :]
            for t in range(halves):
                part = s[t * TILE : (t + 1) * TILE]
                if j < 3:
                    part = part + bias_of((slab - 1 + j) * halves + t, slab)
                st[h, j * frame + t * TILE : j * frame + (t + 1) * TILE, :] = part
                top = jnp.maximum(top, jnp.max(part, axis=0, keepdims=True))
            stat[0, 1, h : h + 1, :] = top

    def transposed_keys(j):
        for h in range(heads):
            kt[h, :, j * frame : (j + 1) * frame] = kall[j, :, hcols(h)].T

    keys_all = st.shape[1]

    def probabilities():
        for d in range(2):
            hk[d].wait_recv()
            scores(2 * d)
        for h in range(heads):
            top = stat[0, 1, h : h + 1, :]
            total = jnp.zeros((1, frame), F32)
            for r in range(0, keys_all, TILE):
                e = jnp.exp(st[h, r : r + TILE, :] - top)
                total = total + jnp.sum(e, axis=0, keepdims=True)
                st[h, r : r + TILE, :] = e
            inv = 1.0 / total
            stat[0, 1, heads + h : heads + h + 1, :] = inv
            for r in range(0, keys_all, TILE):
                p = st[h, r : r + TILE, :] * inv
                st[h, r : r + TILE, :] = p
                pt[h, r : r + TILE, :] = p.astype(BF16)
        for d in range(2):
            ha[d].start()
            transposed_keys(2 * d)

    loads[0].wait()
    loads[1].wait()
    scores(3)
    loads[2].wait()
    scores(1)

    def forward(b):
        for d in range(2):
            xc[b, d, d].wait_recv()
            xf[b, d].start()

    def add_block(c, xslot, b):
        hd_at = head_of((0, -1, 1, 2)[xslot], (0, -1, 1)[b])
        cols = pl.ds(pl.multiple_of(hd_at * frame, frame), frame)
        gacc[rows(c), :] += dot(gbuf[xslot, b, rows(c), :], w[:, cols], ((1,), (1,)))

    forward(0)
    loads[3].wait()
    loads[4].wait()
    gacc[...] = jnp.zeros_like(gacc)
    for c in range(halves):
        add_block(c, 0, 0)

    owner = owner_ref[...]
    texts = owner.shape[1]
    row_i = lax.broadcasted_iota(jnp.int32, (texts, texts), 0)
    col_i = lax.broadcasted_iota(jnp.int32, (texts, texts), 1)
    owner_f = owner.astype(F32)
    owner_col = jnp.sum(jnp.where(row_i == col_i, owner_f, 0.0), axis=1, keepdims=True)
    same = (owner_col == owner_f) & (row_i < col_i)
    rank = jnp.sum(jnp.where(same, 1.0, 0.0), axis=0, keepdims=True).astype(jnp.int32)
    o_rep = owner % reps
    o_seq = owner // reps
    where_to = (((o_seq % 2) * ys + o_seq // 2) * reps + o_rep) * CAP + rank
    slot_i = lax.broadcasted_iota(jnp.int32, place.shape, 0)
    place[...] = jnp.where(slot_i == where_to, 1.0, 0.0).astype(BF16)
    transposed_keys(3)
    transposed_keys(1)

    @pl.when(z == 0)
    def _():
        z_send_later(0)
        probabilities()
        z_send_later(1)

    @pl.when(z == 1)
    def _():
        z_send_later(0)

    for copy in hq:
        copy.start()

    @pl.when(z == 1)
    def _():
        probabilities()

    for d in range(2):
        xc[0, 1 - d, d].wait_recv()
    for e in range(1, 3):
        for c in range(halves):
            add_block(c, e, 0)
    for c in range(halves):
        xf[0, c].wait_recv()
        add_block(c, 3, 0)
    for c in range(halves):
        for d in range(2):
            zc[d][c].wait_recv()
            for e in range(2):
                xc[1 + d, c, e].start()
    for b in range(1, 3):
        forward(b)
    for c in range(halves):
        for b in range(1, 3):
            add_block(c, 0, b)
    for b in range(1, 3):
        for d in range(2):
            xc[b, 1 - d, d].wait_recv()
            for c in range(halves):
                add_block(c, 1 + d, b)
    for b in range(1, 3):
        for c in range(halves):
            xf[b, c].wait_recv()
            add_block(c, 3, b)
    gall[1] = gacc[...].astype(BF16)
    for copy in hg:
        copy.start()

    @pl.when(z == 2)
    def _():
        probabilities()

    def value_part(j, h):
        return dot(pt[h, j * frame : (j + 1) * frame, :], gall[1, :, hcols(h)], ((1,), (0,)))

    def key_part(j, h):
        return dot(ds[h, j * frame : (j + 1) * frame, :], qall[1, :, hcols(h)], ((1,), (0,)))

    half = slots.shape[1] // 2
    block = reps * CAP
    first = [
        remote(slots.at[n, pl.ds((1 - core) * half, half)], trecv1.at[n], t1s.at[n], t1r.at[n], core_dev)
        for n in range(2)
    ]
    second = [
        [
            remote(
                tsum.at[n, pl.ds(((y + d) % ys) * block, block)],
                trecv2.at[n, d - 1],
                t2s.at[n, d - 1],
                t2r.at[n, d - 1],
                y_dev[d - 1],
            )
            for d in range(1, ys)
        ]
        for n in range(2)
    ]
    third = [
        [
            remote(
                t3.at[n, pl.ds(((rep + d) % reps) * CAP, CAP)],
                trecv3.at[n, d - 1],
                t3s.at[n, d - 1],
                t3r.at[n, d - 1],
                r_dev[d - 1],
            )
            for d in range(1, reps)
        ]
        for n in range(2)
    ]

    def text_first(n, part):
        for h in range(heads):
            placed = dot(place[...], part(3, h).astype(BF16), ((1,), (0,)))
            slots[n, :, hcols(h)] = placed.astype(BF16)
        first[n].start()

    def text_second(n):
        first[n].wait_recv()
        mine = slots[n, pl.ds(core * half, half), :].astype(F32)
        tsum[n] = (mine + trecv1[n].astype(F32)).astype(BF16)
        for copy in second[n]:
            copy.start()

    def text_third(n):
        total = tsum[n, pl.ds(y * block, block), :].astype(F32)
        for d in range(1, ys):
            second[n][d - 1].wait_recv()
            total = total + trecv2[n, d - 1].astype(F32)
        t3[n] = total
        for copy in third[n]:
            copy.start()

    def text_last(n, out):
        total = t3[n, pl.ds(rep * CAP, CAP), :]
        for d in range(1, reps):
            third[n][d - 1].wait_recv()
            total = total + trecv3[n, d - 1]
        out[...] = total.astype(BF16)

    delta = [jnp.zeros((1, frame), F32) for _ in range(heads)]

    def dprob(j):
        for h in range(heads):
            for t in range(halves):
                r = j * frame + t * TILE
                part = dot(vall[j, rows(t), hcols(h)], gall[1, :, hcols(h)], ((1,), (1,)))
                dp[h, r : r + TILE, :] = part
                delta[h] = delta[h] + jnp.sum(
                    pt[h, r : r + TILE, :].astype(F32) * part, axis=0, keepdims=True
                )

    def dscore(j):
        for h in range(heads):
            for t in range(halves):
                r = j * frame + t * TILE
                ds[h, r : r + TILE, :] = (
                    st[h, r : r + TILE, :] * (dp[h, r : r + TILE, :] - delta[h])
                ).astype(BF16)

    text_first(0, value_part)
    loads[5].wait()
    loads[6].wait()
    dprob(3)
    dprob(1)
    for d in range(2):
        hv[d].wait_recv()
        dprob(2 * d)
    for h in range(heads):
        stat[1, 1, h : h + 1, :] = delta[h]
    for copy in hd:
        copy.start()
    dscore(3)
    text_first(1, lambda j, h: key_part(j, h) * scale)
    text_second(0)
    for h in range(heads):
        own[0, :, hcols(h)] = value_part(1, h)
    dscore(1)
    text_second(1)
    dscore(0)
    dscore(2)
    for h in range(heads):
        own[1, :, hcols(h)] = key_part(1, h)
    for h in range(heads):
        dqt = dot(kt[h], ds[h], ((1,), (0,))) * scale
        dq_ref[:, hcols(h)] = dqt.T.astype(BF16)

    for d in range(2):
        hq[d].wait_recv()
        ha[d].wait_recv()
        for h in range(heads):
            s = dot(kall[1, :, hcols(h)], qall[2 * d, :, hcols(h)], ((1,), (1,))) * scale
            top = stat[0, 2 * d, h : h + 1, :]
            inv = stat[0, 2 * d, heads + h : heads + h + 1, :]
            for t in range(halves):
                part = s[t * TILE : (t + 1) * TILE] + bias_of(slab * halves + t, (prv, nxt)[d])
                p = jnp.exp(part - top) * inv
                hp[d, h, rows(t), :] = p
                hpt[d, h, rows(t), :] = p.astype(BF16)
    text_third(0)
    for d in range(2):
        hd[d].wait_recv()
        hg[d].wait_recv()
        for h in range(heads):
            g = gall[2 * d, :, hcols(h)]
            own[0, :, hcols(h)] += dot(hpt[d, h], g, ((1,), (0,)))
            dph = dot(vall[1, :, hcols(h)], g, ((1,), (1,)))
            dsh = (hp[d, h] * (dph - stat[1, 2 * d, h : h + 1, :])).astype(BF16)
            own[1, :, hcols(h)] += dot(dsh, qall[2 * d, :, hcols(h)], ((1,), (0,)))
    dv_ref[...] = own[0].astype(BF16)
    dk_ref[...] = (own[1] * scale).astype(BF16)
    text_third(1)
    text_last(0, tvg_ref)
    text_last(1, tkg_ref)

    for copy in sent:
        copy.wait_send()


def hand_over(*refs):
    count = (len(refs) - 2) // 3
    given, taken, held = refs[:count], refs[count : 2 * count], refs[2 * count : 3 * count]
    in_sem, out_sem = refs[3 * count :]
    ins = [pltpu.make_async_copy(given[i], held[i], in_sem.at[i]) for i in range(count)]
    outs = [pltpu.make_async_copy(held[i], taken[i], out_sem.at[i]) for i in range(count)]
    for copy in ins:
        copy.start()
    for i in range(count):
        ins[i].wait()
        outs[i].start()
    for copy in outs:
        copy.wait()


def local(
    seqs,
    reps,
    queries,
    keys,
    values,
    grad_output,
    out_weight,
    text_keys,
    text_values,
    mask_lists,
    text_owner,
):
    frame, width = queries.shape
    texts = text_keys.shape[0]
    heads = width // HD
    ys = seqs // 2
    slots = seqs * reps * CAP
    halves = frame // TILE
    block = reps * CAP
    total = 3 * frame + texts
    grads = jax.ShapeDtypeStruct((frame, width), BF16)
    text_grads = jax.ShapeDtypeStruct((CAP, width), BF16)
    hbm = pl.BlockSpec(memory_space=pltpu.HBM)
    vmem = pl.BlockSpec(memory_space=pltpu.VMEM)
    dma = pltpu.SemaphoreType.DMA
    shapes = (grads, grads, grads, text_grads, text_grads)
    made = pl.pallas_call(
        functools.partial(kernel, seqs, reps),
        out_shape=shapes,
        in_specs=[pl.BlockSpec(memory_space=pltpu.SMEM), vmem] + [hbm] * 7,
        out_specs=(vmem,) * 5,
        scratch_shapes=[
            pltpu.VMEM((3, frame, width), BF16),
            pltpu.VMEM((4, frame, width), BF16),
            pltpu.VMEM((4, frame, width), BF16),
            pltpu.VMEM((3, frame, width), BF16),
            pltpu.VMEM((XS, ZS, frame, width), BF16),
            pltpu.VMEM(out_weight.shape, BF16),
            pltpu.VMEM((frame, width), F32),
            pltpu.VMEM((heads, HD, total), BF16),
            pltpu.VMEM((heads, total, frame), F32),
            pltpu.VMEM((heads, total, frame), BF16),
            pltpu.VMEM((heads, total, frame), F32),
            pltpu.VMEM((heads, total, frame), BF16),
            pltpu.VMEM((2, heads, frame, frame), F32),
            pltpu.VMEM((2, heads, frame, frame), BF16),
            pltpu.VMEM((2, frame, width), F32),
            pltpu.VMEM((2, 3, 8, frame), F32),
            pltpu.VMEM((slots, texts), BF16),
            pltpu.VMEM((2, slots, width), BF16),
            pltpu.VMEM((2, slots // 2, width), BF16),
            pltpu.VMEM((2, slots // 2, width), BF16),
            pltpu.VMEM((2, ys - 1, block, width), BF16),
            pltpu.VMEM((2, block, width), F32),
            pltpu.VMEM((2, reps - 1, CAP, width), F32),
            pltpu.SemaphoreType.REGULAR((2,)),
            dma((7,)),
            dma((2, halves)),
            dma((2, halves)),
            dma((2, 3, halves)),
            dma((2, 3, halves)),
            dma((2, 3)),
            dma((2, 3)),
            dma((6, 2)),
            dma((6, 2)),
            dma((2,)),
            dma((2,)),
            dma((2, ys - 1)),
            dma((2, ys - 1)),
            dma((2, reps - 1)),
            dma((2, reps - 1)),
        ],
        compiler_params=pltpu.CompilerParams(collective_id=0, has_side_effects=True),
    )(
        mask_lists.T,
        text_owner.reshape(1, texts),
        queries,
        keys,
        values,
        grad_output,
        out_weight,
        text_keys,
        text_values,
    )
    return pl.pallas_call(
        hand_over,
        out_shape=shapes,
        in_specs=[pl.BlockSpec(memory_space=pl.ANY)] * 5,
        out_specs=(pl.BlockSpec(memory_space=pl.ANY),) * 5,
        scratch_shapes=[pltpu.VMEM(s.shape, s.dtype) for s in shapes] + [dma((5,)), dma((5,))],
    )(*made)


def solution(mesh):
    rows = P(("seq", "rep"), "head")
    return jax.shard_map(
        functools.partial(local, mesh.shape["seq"], mesh.shape["rep"]),
        mesh=mesh,
        in_specs=(
            rows,
            rows,
            rows,
            rows,
            P("head", None),
            P(None, "head"),
            P(None, "head"),
            P(),
            P(),
        ),
        out_specs=(rows,) * 5,
        check_vma=False,
    )
```

```python
import functools

import jax
import jax.numpy as jnp
from jax import lax
from jax.experimental import pallas as pl
from jax.experimental.pallas import tpu as pltpu
from jax.sharding import PartitionSpec as P

HD = 128
TILE = 128
CAP = 8
CHUNKS = 4
XS = 4
ZS = 3
NEG = -1e30
MESH = pl.DeviceIdType.MESH
F32 = jnp.float32
BF16 = jnp.bfloat16


def dot(a, b, contract):
    return lax.dot_general(a, b, (contract, ((), ())), preferred_element_type=F32)


def kernel(
    seqs,
    reps,
    mask_ref,
    owner_ref,
    q_hbm,
    k_hbm,
    v_hbm,
    g_hbm,
    w_hbm,
    tk_hbm,
    tv_hbm,
    dq_ref,
    dk_ref,
    dv_ref,
    tkg_ref,
    tvg_ref,
    qall,
    kall,
    vall,
    gall,
    gbuf,
    w,
    gacc,
    kt,
    st,
    pt,
    dp,
    ds,
    hp,
    hpt,
    own,
    stat,
    place,
    slots,
    trecv1,
    tsum,
    trecv2,
    t3,
    trecv3,
    ready_z,
    ready_s,
    ready_r,
    local_sem,
    zs,
    zr,
    xss,
    xsr,
    xfs,
    xfr,
    hs,
    hr,
    t1s,
    t1r,
    t2s,
    t2r,
    t3s,
    t3r,
):
    seq = lax.axis_index("seq")
    head = lax.axis_index("head")
    rep = lax.axis_index("rep")
    ys = seqs // 2
    y, core = seq // 2, seq % 2
    x, z = head // ZS, head % ZS
    slabs = seqs * reps
    slab = seq * reps + rep
    frame, width = q_hbm.shape
    heads = width // HD
    halves = frame // TILE
    scale = HD ** (-0.5)

    def head_of(dx, dz):
        return ((x + dx + XS) % XS) * ZS + (z + dz + ZS) % ZS

    z_dev = [{"head": head_of(0, 1)}, {"head": head_of(0, -1)}]
    z_of = [(z + 1) % ZS, (z + ZS - 1) % ZS]
    x_dev = [{"head": head_of(1, 0)}, {"head": head_of(-1, 0)}]
    nxt = (slab + 1) % slabs
    prv = (slab + slabs - 1) % slabs
    s_dev = [
        {"seq": nxt // reps, "rep": nxt % reps},
        {"seq": prv // reps, "rep": prv % reps},
    ]
    core_dev = {"seq": y * 2 + 1 - core}
    y_dev = [{"seq": ((y + d) % ys) * 2 + core} for d in range(1, ys)]
    r_dev = [{"rep": (rep + d) % reps} for d in range(1, reps)]

    loads = [
        pltpu.make_async_copy(src, dst, local_sem.at[i])
        for i, (src, dst) in enumerate(
            [
                (q_hbm, qall.at[1]),
                (tk_hbm, kall.at[3]),
                (k_hbm, kall.at[1]),
                (g_hbm, gbuf.at[0, 0]),
                (w_hbm, w),
                (tv_hbm, vall.at[3]),
                (v_hbm, vall.at[1]),
            ]
        )
    ]
    for load in loads:
        load.start()

    for n in range(2):
        stat[n, 1] = jnp.full(stat.shape[2:], NEG, F32)

    s_rep = [nxt % reps, prv % reps]
    r_rep = [(rep + d) % reps for d in range(1, reps)]
    across = [(z_dev[d], z_of[d] - z, ready_z.at[1 - d]) for d in range(2)]
    across += [(s_dev[d], s_rep[d] - rep, ready_s.at[1 - d]) for d in range(2)]
    across += [(r_dev[d - 1], r_rep[d - 1] - rep, ready_r.at[reps - d - 1]) for d in range(1, reps)]
    barrier = pltpu.get_barrier_semaphore()
    partners = x_dev + [core_dev] + y_dev
    for dev in partners:
        pl.semaphore_signal(barrier, inc=1, device_id=dev, device_id_type=MESH)
    expected = len(partners)
    for dev, above, _ in across:
        expected = expected + jnp.where(above < 0, 1, 0)

        @pl.when(above > 0)
        def _():
            pl.semaphore_signal(barrier, inc=1, device_id=dev, device_id_type=MESH)

    pl.semaphore_wait(barrier, expected)
    for dev, above, sem in across:

        @pl.when(above < 0)
        def _():
            pl.semaphore_signal(sem, inc=1, device_id=dev, device_id_type=MESH)

    sent = []

    def remote(src, dst, ssem, rsem, dev):
        copy = pltpu.make_async_remote_copy(
            src_ref=src, dst_ref=dst, send_sem=ssem, recv_sem=rsem, device_id=dev, device_id_type=MESH
        )
        sent.append(copy)
        return copy

    def rows(c):
        return pl.ds(c * TILE, TILE)

    def hcols(h):
        return slice(h * HD, (h + 1) * HD)

    step = frame // CHUNKS

    def part(c):
        return pl.ds(c * step, step)

    zc = [
        [
            remote(g_hbm.at[part(c)], gbuf.at[0, 1 + d, part(c)], zs.at[d, c], zr.at[d, c], z_dev[d])
            for c in range(CHUNKS)
        ]
        for d in range(2)
    ]
    xc = {}
    xf = {}
    for b in range(3):
        for c in range(CHUNKS):
            for d in range(2):
                src = g_hbm.at[part(c)] if b == 0 else gbuf.at[0, b, part(c)]
                xc[b, c, d] = remote(
                    src, gbuf.at[1 + d, b, part(c)], xss.at[d, b, c], xsr.at[d, b, c], x_dev[d]
                )
            d = c % 2
            xf[b, c] = remote(
                gbuf.at[1 + d, b, part(c)], gbuf.at[3, b, part(c)], xfs.at[b, c], xfr.at[b, c], x_dev[d]
            )

    def halo(n, src, dst):
        return [remote(src, dst.at[2 * d], hs.at[n, d], hr.at[n, d], s_dev[d]) for d in range(2)]

    hk = halo(0, k_hbm, kall)
    hv = halo(1, v_hbm, vall)
    hq = halo(2, q_hbm, qall)
    hg = halo(3, gall.at[1], gall)
    ha = halo(4, stat.at[0, 1], stat.at[0])
    hd = halo(5, stat.at[1, 1], stat.at[1])

    def z_send(d):
        for c in range(CHUNKS):
            zc[d][c].start()

    def z_send_later(d):
        pl.semaphore_wait(ready_z.at[d], 1)
        z_send(d)

    for d in range(2):

        @pl.when(z_of[d] < z)
        def _():
            z_send(d)

    for c in range(CHUNKS):
        for d in range(2):
            xc[0, c, d].start()

    lane = lax.broadcasted_iota(jnp.int32, (1, frame), 1)

    def bias_of(tile, of_slab):
        bias = jnp.zeros((1, frame), F32)
        for c in range(halves):
            hit = mask_ref[0, of_slab * halves + c] == tile
            for i in range(1, 3):
                hit = hit | (mask_ref[i, of_slab * halves + c] == tile)
            level = jnp.where(hit, jnp.float32(0.0), jnp.float32(NEG))
            bias = jnp.where(lane // TILE == c, level, bias)
        return bias

    def scores(j):
        for h in range(heads):
            s = dot(kall[j, :, hcols(h)], qall[1, :, hcols(h)], ((1,), (1,))) * scale
            top = stat[0, 1, h : h + 1, :]
            for t in range(halves):
                part = s[t * TILE : (t + 1) * TILE]
                if j < 3:
                    part = part + bias_of((slab - 1 + j) * halves + t, slab)
                st[h, j * frame + t * TILE : j * frame + (t + 1) * TILE, :] = part
                top = jnp.maximum(top, jnp.max(part, axis=0, keepdims=True))
            stat[0, 1, h : h + 1, :] = top

    def transposed_keys(j):
        for h in range(heads):
            kt[h, :, j * frame : (j + 1) * frame] = kall[j, :, hcols(h)].T

    keys_all = st.shape[1]

    def probabilities():
        for d in range(2):
            hk[d].wait_recv()
            scores(2 * d)
        for h in range(heads):
            top = stat[0, 1, h : h + 1, :]
            total = jnp.zeros((1, frame), F32)
            for r in range(0, keys_all, TILE):
                e = jnp.exp(st[h, r : r + TILE, :] - top)
                total = total + jnp.sum(e, axis=0, keepdims=True)
                st[h, r : r + TILE, :] = e
            inv = 1.0 / total
            stat[0, 1, heads + h : heads + h + 1, :] = inv
            for r in range(0, keys_all, TILE):
                p = st[h, r : r + TILE, :] * inv
                st[h, r : r + TILE, :] = p
                pt[h, r : r + TILE, :] = p.astype(BF16)
        for d in range(2):
            ha[d].start()
            transposed_keys(2 * d)

    loads[0].wait()
    loads[1].wait()
    scores(3)
    loads[2].wait()
    scores(1)

    for d in range(2):

        @pl.when(s_rep[d] > rep)
        def _():
            pl.semaphore_wait(ready_s.at[d], 1)

    @pl.when(z < ZS - 1)
    def _():
        for copy in hk + hv:
            copy.start()

    def forward(b, c):
        xc[b, c, c % 2].wait_recv()
        xf[b, c].start()

    def add_block(xslot, b):
        hd_at = head_of((0, -1, 1, 2)[xslot], (0, -1, 1)[b])
        cols = pl.ds(pl.multiple_of(hd_at * frame, frame), frame)
        gacc[...] += dot(gbuf[xslot, b], w[:, cols], ((1,), (1,)))

    def pump(blocks, after):
        for c in range(CHUNKS):
            for b in blocks:
                zc[b - 1][c].wait_recv()
                for d in range(2):
                    xc[b, c, d].start()
            if c > 0:
                for b in blocks:
                    forward(b, c - 1)
            for copy in after.get(c, ()):
                copy.start()
        for b in blocks:
            forward(b, CHUNKS - 1)

    def drain(b):
        if b > 0:
            add_block(0, b)
        for d in range(2):
            for c in range(CHUNKS):
                if c % 2 != d:
                    xc[b, c, d].wait_recv()
            add_block(1 + d, b)
        for c in range(CHUNKS):
            xf[b, c].wait_recv()
        add_block(3, b)

    for c in range(CHUNKS):
        forward(0, c)
    loads[3].wait()
    loads[4].wait()
    gacc[...] = jnp.zeros_like(gacc)
    add_block(0, 0)

    owner = owner_ref[...]
    texts = owner.shape[1]
    row_i = lax.broadcasted_iota(jnp.int32, (texts, texts), 0)
    col_i = lax.broadcasted_iota(jnp.int32, (texts, texts), 1)
    owner_f = owner.astype(F32)
    owner_col = jnp.sum(jnp.where(row_i == col_i, owner_f, 0.0), axis=1, keepdims=True)
    same = (owner_col == owner_f) & (row_i < col_i)
    rank = jnp.sum(jnp.where(same, 1.0, 0.0), axis=0, keepdims=True).astype(jnp.int32)
    o_rep = owner % reps
    o_seq = owner // reps
    where_to = (((o_seq % 2) * ys + o_seq // 2) * reps + o_rep) * CAP + rank
    slot_i = lax.broadcasted_iota(jnp.int32, place.shape, 0)
    place[...] = jnp.where(slot_i == where_to, 1.0, 0.0).astype(BF16)
    transposed_keys(3)
    transposed_keys(1)

    @pl.when(z == 0)
    def _():
        z_send_later(0)
        probabilities()
        z_send_later(1)
        for copy in hq:
            copy.start()
        drain(0)
        pump([2], {})
        drain(2)
        pump([1], {})
        drain(1)

    @pl.when(z == 1)
    def _():
        z_send_later(0)
        for copy in hq:
            copy.start()
        probabilities()
        drain(0)
        pump([1], {})
        drain(1)
        pump([2], {})
        drain(2)

    @pl.when(z == 2)
    def _():
        drain(0)
        pump([1, 2], {1: hk, 3: hv})
        drain(1)
        drain(2)
        for copy in hq:
            copy.start()

    gall[1] = gacc[...].astype(BF16)
    for copy in hg:
        copy.start()

    @pl.when(z == 2)
    def _():
        probabilities()

    def value_part(j, h):
        return dot(pt[h, j * frame : (j + 1) * frame, :], gall[1, :, hcols(h)], ((1,), (0,)))

    def key_part(j, h):
        return dot(ds[h, j * frame : (j + 1) * frame, :], qall[1, :, hcols(h)], ((1,), (0,)))

    half = slots.shape[1] // 2
    block = reps * CAP
    first = [
        remote(slots.at[n, pl.ds((1 - core) * half, half)], trecv1.at[n], t1s.at[n], t1r.at[n], core_dev)
        for n in range(2)
    ]
    second = [
        [
            remote(
                tsum.at[n, pl.ds(((y + d) % ys) * block, block)],
                trecv2.at[n, d - 1],
                t2s.at[n, d - 1],
                t2r.at[n, d - 1],
                y_dev[d - 1],
            )
            for d in range(1, ys)
        ]
        for n in range(2)
    ]
    third = [
        [
            remote(
                t3.at[n, pl.ds(((rep + d) % reps) * CAP, CAP)],
                trecv3.at[n, d - 1],
                t3s.at[n, d - 1],
                t3r.at[n, d - 1],
                r_dev[d - 1],
            )
            for d in range(1, reps)
        ]
        for n in range(2)
    ]

    def text_first(n, made):
        halved = [made(3, h).astype(BF16) for h in range(heads)]
        for k in (1 - core, core):
            to = pl.ds(pl.multiple_of(k * half, half), half)
            for h in range(heads):
                slots[n, to, hcols(h)] = dot(place[to, :], halved[h], ((1,), (0,))).astype(BF16)
            if k is not core:
                first[n].start()

    def text_second(n):
        first[n].wait_recv()
        mine = slots[n, pl.ds(core * half, half), :].astype(F32)
        tsum[n] = (mine + trecv1[n].astype(F32)).astype(BF16)
        for copy in second[n]:
            copy.start()

    def text_third(n):
        total = tsum[n, pl.ds(y * block, block), :].astype(F32)
        for d in range(1, ys):
            second[n][d - 1].wait_recv()
            total = total + trecv2[n, d - 1].astype(F32)
        t3[n] = total
        if n == 0:
            for d in range(1, reps):

                @pl.when(r_rep[d - 1] > rep)
                def _():
                    pl.semaphore_wait(ready_r.at[d - 1], 1)

        for copy in third[n]:
            copy.start()

    def text_last(n, out):
        total = t3[n, pl.ds(rep * CAP, CAP), :]
        for d in range(1, reps):
            third[n][d - 1].wait_recv()
            total = total + trecv3[n, d - 1]
        out[...] = total.astype(BF16)

    delta = [jnp.zeros((1, frame), F32) for _ in range(heads)]

    def dprob(j):
        for h in range(heads):
            for t in range(halves):
                r = j * frame + t * TILE
                part = dot(vall[j, rows(t), hcols(h)], gall[1, :, hcols(h)], ((1,), (1,)))
                dp[h, r : r + TILE, :] = part
                delta[h] = delta[h] + jnp.sum(
                    pt[h, r : r + TILE, :].astype(F32) * part, axis=0, keepdims=True
                )

    def dscore(j):
        for h in range(heads):
            for t in range(halves):
                r = j * frame + t * TILE
                ds[h, r : r + TILE, :] = (
                    st[h, r : r + TILE, :] * (dp[h, r : r + TILE, :] - delta[h])
                ).astype(BF16)

    text_first(0, value_part)
    loads[5].wait()
    loads[6].wait()
    dprob(3)
    dprob(1)
    for d in range(2):
        hv[d].wait_recv()
        dprob(2 * d)
    for h in range(heads):
        stat[1, 1, h : h + 1, :] = delta[h]
    for copy in hd:
        copy.start()
    dscore(3)
    text_first(1, lambda j, h: key_part(j, h) * scale)
    text_second(0)
    for h in range(heads):
        own[0, :, hcols(h)] = value_part(1, h)
    dscore(1)
    text_second(1)
    dscore(0)
    dscore(2)
    for h in range(heads):
        own[1, :, hcols(h)] = key_part(1, h)
    for h in range(heads):
        dqt = dot(kt[h], ds[h], ((1,), (0,))) * scale
        dq_ref[:, hcols(h)] = dqt.T.astype(BF16)

    for d in range(2):
        hq[d].wait_recv()
        ha[d].wait_recv()
        for h in range(heads):
            s = dot(kall[1, :, hcols(h)], qall[2 * d, :, hcols(h)], ((1,), (1,))) * scale
            top = stat[0, 2 * d, h : h + 1, :]
            inv = stat[0, 2 * d, heads + h : heads + h + 1, :]
            for t in range(halves):
                part = s[t * TILE : (t + 1) * TILE] + bias_of(slab * halves + t, (prv, nxt)[d])
                p = jnp.exp(part - top) * inv
                hp[d, h, rows(t), :] = p
                hpt[d, h, rows(t), :] = p.astype(BF16)
    text_third(0)
    for d in range(2):
        hd[d].wait_recv()
        hg[d].wait_recv()
        for h in range(heads):
            g = gall[2 * d, :, hcols(h)]
            own[0, :, hcols(h)] += dot(hpt[d, h], g, ((1,), (0,)))
            dph = dot(vall[1, :, hcols(h)], g, ((1,), (1,)))
            dsh = (hp[d, h] * (dph - stat[1, 2 * d, h : h + 1, :])).astype(BF16)
            own[1, :, hcols(h)] += dot(dsh, qall[2 * d, :, hcols(h)], ((1,), (0,)))
    dv_ref[...] = own[0].astype(BF16)
    dk_ref[...] = (own[1] * scale).astype(BF16)
    text_third(1)
    text_last(0, tvg_ref)
    text_last(1, tkg_ref)

    for copy in sent:
        copy.wait_send()


def hand_over(*refs):
    count = (len(refs) - 2) // 3
    given, taken, held = refs[:count], refs[count : 2 * count], refs[2 * count : 3 * count]
    in_sem, out_sem = refs[3 * count :]
    ins = [pltpu.make_async_copy(given[i], held[i], in_sem.at[i]) for i in range(count)]
    outs = [pltpu.make_async_copy(held[i], taken[i], out_sem.at[i]) for i in range(count)]
    for copy in ins:
        copy.start()
    for i in range(count):
        ins[i].wait()
        outs[i].start()
    for copy in outs:
        copy.wait()


def local(
    seqs,
    reps,
    queries,
    keys,
    values,
    grad_output,
    out_weight,
    text_keys,
    text_values,
    mask_lists,
    text_owner,
):
    frame, width = queries.shape
    texts = text_keys.shape[0]
    heads = width // HD
    ys = seqs // 2
    slots = seqs * reps * CAP
    block = reps * CAP
    total = 3 * frame + texts
    grads = jax.ShapeDtypeStruct((frame, width), BF16)
    text_grads = jax.ShapeDtypeStruct((CAP, width), BF16)
    hbm = pl.BlockSpec(memory_space=pltpu.HBM)
    vmem = pl.BlockSpec(memory_space=pltpu.VMEM)
    dma = pltpu.SemaphoreType.DMA
    shapes = (grads, grads, grads, text_grads, text_grads)
    made = pl.pallas_call(
        functools.partial(kernel, seqs, reps),
        out_shape=shapes,
        in_specs=[pl.BlockSpec(memory_space=pltpu.SMEM), vmem] + [hbm] * 7,
        out_specs=(vmem,) * 5,
        scratch_shapes=[
            pltpu.VMEM((3, frame, width), BF16),
            pltpu.VMEM((4, frame, width), BF16),
            pltpu.VMEM((4, frame, width), BF16),
            pltpu.VMEM((3, frame, width), BF16),
            pltpu.VMEM((XS, ZS, frame, width), BF16),
            pltpu.VMEM(out_weight.shape, BF16),
            pltpu.VMEM((frame, width), F32),
            pltpu.VMEM((heads, HD, total), BF16),
            pltpu.VMEM((heads, total, frame), F32),
            pltpu.VMEM((heads, total, frame), BF16),
            pltpu.VMEM((heads, total, frame), F32),
            pltpu.VMEM((heads, total, frame), BF16),
            pltpu.VMEM((2, heads, frame, frame), F32),
            pltpu.VMEM((2, heads, frame, frame), BF16),
            pltpu.VMEM((2, frame, width), F32),
            pltpu.VMEM((2, 3, 8, frame), F32),
            pltpu.VMEM((slots, texts), BF16),
            pltpu.VMEM((2, slots, width), BF16),
            pltpu.VMEM((2, slots // 2, width), BF16),
            pltpu.VMEM((2, slots // 2, width), BF16),
            pltpu.VMEM((2, ys - 1, block, width), BF16),
            pltpu.VMEM((2, block, width), F32),
            pltpu.VMEM((2, reps - 1, CAP, width), F32),
            pltpu.SemaphoreType.REGULAR((2,)),
            pltpu.SemaphoreType.REGULAR((2,)),
            pltpu.SemaphoreType.REGULAR((reps - 1,)),
            dma((7,)),
            dma((2, CHUNKS)),
            dma((2, CHUNKS)),
            dma((2, 3, CHUNKS)),
            dma((2, 3, CHUNKS)),
            dma((3, CHUNKS)),
            dma((3, CHUNKS)),
            dma((6, 2)),
            dma((6, 2)),
            dma((2,)),
            dma((2,)),
            dma((2, ys - 1)),
            dma((2, ys - 1)),
            dma((2, reps - 1)),
            dma((2, reps - 1)),
        ],
        compiler_params=pltpu.CompilerParams(collective_id=0, has_side_effects=True),
    )(
        mask_lists.T,
        text_owner.reshape(1, texts),
        queries,
        keys,
        values,
        grad_output,
        out_weight,
        text_keys,
        text_values,
    )
    return pl.pallas_call(
        hand_over,
        out_shape=shapes,
        in_specs=[pl.BlockSpec(memory_space=pl.ANY)] * 5,
        out_specs=(pl.BlockSpec(memory_space=pl.ANY),) * 5,
        scratch_shapes=[pltpu.VMEM(s.shape, s.dtype) for s in shapes] + [dma((5,)), dma((5,))],
    )(*made)


def solution(mesh):
    rows = P(("seq", "rep"), "head")
    return jax.shard_map(
        functools.partial(local, mesh.shape["seq"], mesh.shape["rep"]),
        mesh=mesh,
        in_specs=(
            rows,
            rows,
            rows,
            rows,
            P("head", None),
            P(None, "head"),
            P(None, "head"),
            P(),
            P(),
        ),
        out_specs=(rows,) * 5,
        check_vma=False,
    )
```

```python
import functools

import jax
import jax.numpy as jnp
from jax import lax
from jax.experimental import pallas as pl
from jax.experimental.pallas import tpu as pltpu
from jax.sharding import PartitionSpec as P

HD = 128
TILE = 128
CAP = 8
XS = 4
ZS = 3
NEG = -1e30
MESH = pl.DeviceIdType.MESH
F32 = jnp.float32
BF16 = jnp.bfloat16


def dot(a, b, contract):
    return lax.dot_general(a, b, (contract, ((), ())), preferred_element_type=F32)


def kernel(
    seqs,
    reps,
    mask_ref,
    owner_ref,
    q_hbm,
    k_hbm,
    v_hbm,
    g_hbm,
    w_hbm,
    tk_hbm,
    tv_hbm,
    dq_ref,
    dk_ref,
    dv_ref,
    tkg_ref,
    tvg_ref,
    qall,
    kall,
    vall,
    gall,
    gbuf,
    w,
    gacc,
    kt,
    st,
    pt,
    vt,
    att,
    ds,
    hp,
    hpt,
    own,
    stat,
    place,
    slots,
    trecv1,
    tsum,
    trecv2,
    t3,
    trecv3,
    ready,
    local_sem,
    zs,
    zr,
    xss,
    xsr,
    xfs,
    xfr,
    hs,
    hr,
    t1s,
    t1r,
    t2s,
    t2r,
    t3s,
    t3r,
):
    seq = lax.axis_index("seq")
    head = lax.axis_index("head")
    rep = lax.axis_index("rep")
    ys = seqs // 2
    y, core = seq // 2, seq % 2
    x, z = head // ZS, head % ZS
    slabs = seqs * reps
    slab = seq * reps + rep
    frame, width = q_hbm.shape
    heads = width // HD
    halves = frame // TILE
    scale = HD ** (-0.5)

    def head_of(dx, dz):
        return ((x + dx + XS) % XS) * ZS + (z + dz + ZS) % ZS

    z_dev = [{"head": head_of(0, 1)}, {"head": head_of(0, -1)}]
    z_of = [(z + 1) % ZS, (z + ZS - 1) % ZS]
    x_dev = [{"head": head_of(1, 0)}, {"head": head_of(-1, 0)}]
    nxt = (slab + 1) % slabs
    prv = (slab + slabs - 1) % slabs
    s_dev = [
        {"seq": nxt // reps, "rep": nxt % reps},
        {"seq": prv // reps, "rep": prv % reps},
    ]
    core_dev = {"seq": y * 2 + 1 - core}
    y_dev = [{"seq": ((y + d) % ys) * 2 + core} for d in range(1, ys)]
    r_dev = [{"rep": (rep + d) % reps} for d in range(1, reps)]

    loads = [
        pltpu.make_async_copy(src, dst, local_sem.at[i])
        for i, (src, dst) in enumerate(
            [
                (q_hbm, qall.at[1]),
                (tk_hbm, kall.at[3]),
                (k_hbm, kall.at[1]),
                (g_hbm, gbuf.at[0, 0]),
                (w_hbm, w),
                (tv_hbm, vall.at[3]),
                (v_hbm, vall.at[1]),
            ]
        )
    ]
    for load in loads:
        load.start()

    for n in range(2):
        stat[n, 1] = jnp.full(stat.shape[2:], NEG, F32)

    barrier = pltpu.get_barrier_semaphore()
    partners = x_dev + s_dev + [core_dev] + y_dev + r_dev
    for dev in partners:
        pl.semaphore_signal(barrier, inc=1, device_id=dev, device_id_type=MESH)
    pl.semaphore_wait(barrier, len(partners) + z)
    for d in range(2):

        @pl.when(z_of[d] > z)
        def _():
            pl.semaphore_signal(barrier, inc=1, device_id=z_dev[d], device_id_type=MESH)

        @pl.when(z_of[d] < z)
        def _():
            pl.semaphore_signal(ready.at[1 - d], inc=1, device_id=z_dev[d], device_id_type=MESH)

    sent = []

    def remote(src, dst, ssem, rsem, dev):
        copy = pltpu.make_async_remote_copy(
            src_ref=src, dst_ref=dst, send_sem=ssem, recv_sem=rsem, device_id=dev, device_id_type=MESH
        )
        sent.append(copy)
        return copy

    def rows(c):
        return pl.ds(c * TILE, TILE)

    def hcols(h):
        return slice(h * HD, (h + 1) * HD)

    hrows = hcols

    zc = [
        [
            remote(g_hbm.at[rows(c)], gbuf.at[0, 1 + d, rows(c)], zs.at[d, c], zr.at[d, c], z_dev[d])
            for c in range(halves)
        ]
        for d in range(2)
    ]
    xc = {}
    xf = {}
    for b in range(3):
        for c in range(halves):
            for d in range(2):
                src = g_hbm.at[rows(c)] if b == 0 else gbuf.at[0, b, rows(c)]
                xc[b, c, d] = remote(
                    src, gbuf.at[1 + d, b, rows(c)], xss.at[d, b, c], xsr.at[d, b, c], x_dev[d]
                )
        for d in range(2):
            xf[b, d] = remote(
                gbuf.at[1 + d, b, rows(d)], gbuf.at[3, b, rows(d)], xfs.at[d, b], xfr.at[d, b], x_dev[d]
            )

    def halo(n, src, dst):
        return [remote(src, dst.at[2 * d], hs.at[n, d], hr.at[n, d], s_dev[d]) for d in range(2)]

    hk = halo(0, k_hbm, kall)
    hv = halo(1, v_hbm, vall)
    hq = halo(2, q_hbm, qall)
    hg = halo(3, gall.at[1], gall)
    ha = halo(4, stat.at[0, 1], stat.at[0])
    hd = halo(5, stat.at[1, 1], stat.at[1])

    def z_send(d):
        for c in range(halves):
            zc[d][c].start()

    def z_send_later(d):
        pl.semaphore_wait(ready.at[d], 1)
        z_send(d)

    for d in range(2):

        @pl.when(z_of[d] < z)
        def _():
            z_send(d)

    for c in range(halves):
        for d in range(2):
            xc[0, c, d].start()
    for copy in hk + hv:
        copy.start()

    lane = lax.broadcasted_iota(jnp.int32, (1, frame), 1)

    def bias_of(tile, of_slab):
        bias = jnp.zeros((1, frame), F32)
        for c in range(halves):
            hit = mask_ref[0, of_slab * halves + c] == tile
            for i in range(1, 3):
                hit = hit | (mask_ref[i, of_slab * halves + c] == tile)
            level = jnp.where(hit, jnp.float32(0.0), jnp.float32(NEG))
            bias = jnp.where(lane // TILE == c, level, bias)
        return bias

    def scores(j):
        for h in range(heads):
            s = dot(kall[j, :, hcols(h)], qall[1, :, hcols(h)], ((1,), (1,))) * scale
            top = stat[0, 1, h : h + 1, :]
            for t in range(halves):
                part = s[t * TILE : (t + 1) * TILE]
                if j < 3:
                    part = part + bias_of((slab - 1 + j) * halves + t, slab)
                st[h, j * frame + t * TILE : j * frame + (t + 1) * TILE, :] = part
                top = jnp.maximum(top, jnp.max(part, axis=0, keepdims=True))
            stat[0, 1, h : h + 1, :] = top

    def transposed_keys(j):
        for h in range(heads):
            kt[h, :, j * frame : (j + 1) * frame] = kall[j, :, hcols(h)].T

    keys_all = st.shape[1]

    def probabilities():
        for d in range(2):
            hk[d].wait_recv()
            scores(2 * d)
        for h in range(heads):
            top = stat[0, 1, h : h + 1, :]
            total = jnp.zeros((1, frame), F32)
            for r in range(0, keys_all, TILE):
                e = jnp.exp(st[h, r : r + TILE, :] - top)
                total = total + jnp.sum(e, axis=0, keepdims=True)
                st[h, r : r + TILE, :] = e
            inv = 1.0 / total
            stat[0, 1, heads + h : heads + h + 1, :] = inv
            for r in range(0, keys_all, TILE):
                p = st[h, r : r + TILE, :] * inv
                st[h, r : r + TILE, :] = p
                pt[h, r : r + TILE, :] = p.astype(BF16)
        for d in range(2):
            ha[d].start()
            transposed_keys(2 * d)

    loads[0].wait()
    loads[1].wait()
    scores(3)
    loads[2].wait()
    scores(1)

    def forward(b):
        for d in range(2):
            xc[b, d, d].wait_recv()
            xf[b, d].start()

    def add_block(c, xslot, b):
        hd_at = head_of((0, -1, 1, 2)[xslot], (0, -1, 1)[b])
        cols = pl.ds(pl.multiple_of(hd_at * frame, frame), frame)
        gacc[:, c * TILE : (c + 1) * TILE] += dot(w[:, cols], gbuf[xslot, b, rows(c), :], ((1,), (1,)))

    forward(0)
    loads[3].wait()
    loads[4].wait()
    gacc[...] = jnp.zeros_like(gacc)
    for c in range(halves):
        add_block(c, 0, 0)

    owner = owner_ref[...]
    texts = owner.shape[1]
    row_i = lax.broadcasted_iota(jnp.int32, (texts, texts), 0)
    col_i = lax.broadcasted_iota(jnp.int32, (texts, texts), 1)
    owner_f = owner.astype(F32)
    owner_col = jnp.sum(jnp.where(row_i == col_i, owner_f, 0.0), axis=1, keepdims=True)
    same = (owner_col == owner_f) & (row_i < col_i)
    rank = jnp.sum(jnp.where(same, 1.0, 0.0), axis=0, keepdims=True).astype(jnp.int32)
    o_rep = owner % reps
    o_seq = owner // reps
    where_to = (((o_seq % 2) * ys + o_seq // 2) * reps + o_rep) * CAP + rank
    slot_i = lax.broadcasted_iota(jnp.int32, place.shape, 0)
    place[...] = jnp.where(slot_i == where_to, 1.0, 0.0).astype(BF16)
    transposed_keys(3)
    transposed_keys(1)

    @pl.when(z == 0)
    def _():
        z_send_later(0)
        probabilities()
        z_send_later(1)

    @pl.when(z == 1)
    def _():
        z_send_later(0)

    for copy in hq:
        copy.start()

    @pl.when(z == 1)
    def _():
        probabilities()

    for d in range(2):
        xc[0, 1 - d, d].wait_recv()
    for e in range(1, 3):
        for c in range(halves):
            add_block(c, e, 0)
    for c in range(halves):
        xf[0, c].wait_recv()
        add_block(c, 3, 0)
    for c in range(halves):
        for d in range(2):
            zc[d][c].wait_recv()
            for e in range(2):
                xc[1 + d, c, e].start()
    @pl.when(z == 2)
    def _():
        probabilities()

    for b in range(1, 3):
        forward(b)
    for c in range(halves):
        for b in range(1, 3):
            add_block(c, 0, b)
    loads[5].wait()
    loads[6].wait()
    for d in range(2):
        hv[d].wait_recv()
    for h in range(heads):
        for j in range(4):
            vt[h, :, j * frame : (j + 1) * frame] = vall[j, :, hcols(h)].T
        att[h] = dot(vt[h], pt[h], ((1,), (0,)))
    for b in range(1, 3):
        for d in range(2):
            xc[b, 1 - d, d].wait_recv()
            for c in range(halves):
                add_block(c, 1 + d, b)
    for b in range(1, 3):
        for c in range(halves):
            xf[b, c].wait_recv()
            add_block(c, 3, b)
    gall[1] = gacc[...].astype(BF16)
    for copy in hg:
        copy.start()

    def value_part(j, h):
        return dot(pt[h, j * frame : (j + 1) * frame, :], gall[1, hrows(h), :], ((1,), (1,)))

    def key_part(j, h):
        return dot(ds[h, j * frame : (j + 1) * frame, :], qall[1, :, hcols(h)], ((1,), (0,)))

    half = slots.shape[1] // 2
    block = reps * CAP
    first = [
        remote(slots.at[n, pl.ds((1 - core) * half, half)], trecv1.at[n], t1s.at[n], t1r.at[n], core_dev)
        for n in range(2)
    ]
    second = [
        [
            remote(
                tsum.at[n, pl.ds(((y + d) % ys) * block, block)],
                trecv2.at[n, d - 1],
                t2s.at[n, d - 1],
                t2r.at[n, d - 1],
                y_dev[d - 1],
            )
            for d in range(1, ys)
        ]
        for n in range(2)
    ]
    third = [
        [
            remote(
                t3.at[n, pl.ds(((rep + d) % reps) * CAP, CAP)],
                trecv3.at[n, d - 1],
                t3s.at[n, d - 1],
                t3r.at[n, d - 1],
                r_dev[d - 1],
            )
            for d in range(1, reps)
        ]
        for n in range(2)
    ]

    def text_first(n, part):
        for h in range(heads):
            placed = dot(place[...], part(3, h).astype(BF16), ((1,), (0,)))
            slots[n, :, hcols(h)] = placed.astype(BF16)
        first[n].start()

    def text_second(n):
        first[n].wait_recv()
        mine = slots[n, pl.ds(core * half, half), :].astype(F32)
        tsum[n] = (mine + trecv1[n].astype(F32)).astype(BF16)
        for d in sorted(range(1, ys), key=lambda d: -min(d, ys - d)):
            second[n][d - 1].start()

    def text_third(n):
        total = tsum[n, pl.ds(y * block, block), :].astype(F32)
        for d in range(1, ys):
            second[n][d - 1].wait_recv()
            total = total + trecv2[n, d - 1].astype(F32)
        t3[n] = total
        for copy in third[n]:
            copy.start()

    def text_last(n, out):
        total = t3[n, pl.ds(rep * CAP, CAP), :]
        for d in range(1, reps):
            third[n][d - 1].wait_recv()
            total = total + trecv3[n, d - 1]
        out[...] = total.astype(BF16)

    delta = []
    for h in range(heads):
        delta.append(jnp.sum(gall[1, hrows(h), :].astype(F32) * att[h], axis=0, keepdims=True))
        stat[1, 1, h : h + 1, :] = delta[h]
    for copy in hd:
        copy.start()

    def dscore(j):
        for h in range(heads):
            for t in range(halves):
                r = j * frame + t * TILE
                part = dot(vall[j, rows(t), hcols(h)], gall[1, hrows(h), :], ((1,), (0,)))
                ds[h, r : r + TILE, :] = (st[h, r : r + TILE, :] * (part - delta[h])).astype(BF16)

    text_first(0, value_part)
    dscore(3)
    text_first(1, lambda j, h: key_part(j, h) * scale)
    text_second(0)
    dscore(1)
    text_second(1)
    for h in range(heads):
        own[0, :, hcols(h)] = value_part(1, h)
    dscore(0)
    dscore(2)
    for h in range(heads):
        own[1, :, hcols(h)] = key_part(1, h)
    for h in range(heads):
        dqt = dot(kt[h], ds[h], ((1,), (0,))) * scale
        dq_ref[:, hcols(h)] = dqt.T.astype(BF16)
    text_third(0)

    for d in range(2):
        hq[d].wait_recv()
        ha[d].wait_recv()
        for h in range(heads):
            s = dot(kall[1, :, hcols(h)], qall[2 * d, :, hcols(h)], ((1,), (1,))) * scale
            top = stat[0, 2 * d, h : h + 1, :]
            inv = stat[0, 2 * d, heads + h : heads + h + 1, :]
            for t in range(halves):
                part = s[t * TILE : (t + 1) * TILE] + bias_of(slab * halves + t, (prv, nxt)[d])
                p = jnp.exp(part - top) * inv
                hp[d, h, rows(t), :] = p
                hpt[d, h, rows(t), :] = p.astype(BF16)
    text_third(1)
    for d in range(2):
        hd[d].wait_recv()
        hg[d].wait_recv()
        for h in range(heads):
            g = gall[2 * d, hrows(h), :]
            own[0, :, hcols(h)] += dot(hpt[d, h], g, ((1,), (1,)))
            dph = dot(vall[1, :, hcols(h)], g, ((1,), (0,)))
            dsh = (hp[d, h] * (dph - stat[1, 2 * d, h : h + 1, :])).astype(BF16)
            own[1, :, hcols(h)] += dot(dsh, qall[2 * d, :, hcols(h)], ((1,), (0,)))
    dv_ref[...] = own[0].astype(BF16)
    dk_ref[...] = (own[1] * scale).astype(BF16)
    text_last(0, tvg_ref)
    text_last(1, tkg_ref)

    for copy in sent:
        copy.wait_send()


def hand_over(*refs):
    count = (len(refs) - 2) // 3
    given, taken, held = refs[:count], refs[count : 2 * count], refs[2 * count : 3 * count]
    in_sem, out_sem = refs[3 * count :]
    ins = [pltpu.make_async_copy(given[i], held[i], in_sem.at[i]) for i in range(count)]
    outs = [pltpu.make_async_copy(held[i], taken[i], out_sem.at[i]) for i in range(count)]
    for copy in ins:
        copy.start()
    for i in range(count):
        ins[i].wait()
        outs[i].start()
    for copy in outs:
        copy.wait()


def local(
    seqs,
    reps,
    queries,
    keys,
    values,
    grad_output,
    out_weight,
    text_keys,
    text_values,
    mask_lists,
    text_owner,
):
    frame, width = queries.shape
    texts = text_keys.shape[0]
    heads = width // HD
    ys = seqs // 2
    slots = seqs * reps * CAP
    halves = frame // TILE
    block = reps * CAP
    total = 3 * frame + texts
    grads = jax.ShapeDtypeStruct((frame, width), BF16)
    text_grads = jax.ShapeDtypeStruct((CAP, width), BF16)
    hbm = pl.BlockSpec(memory_space=pltpu.HBM)
    vmem = pl.BlockSpec(memory_space=pltpu.VMEM)
    dma = pltpu.SemaphoreType.DMA
    shapes = (grads, grads, grads, text_grads, text_grads)
    made = pl.pallas_call(
        functools.partial(kernel, seqs, reps),
        out_shape=shapes,
        in_specs=[pl.BlockSpec(memory_space=pltpu.SMEM), vmem] + [hbm] * 7,
        out_specs=(vmem,) * 5,
        scratch_shapes=[
            pltpu.VMEM((3, frame, width), BF16),
            pltpu.VMEM((4, frame, width), BF16),
            pltpu.VMEM((4, frame, width), BF16),
            pltpu.VMEM((3, frame, width), BF16),
            pltpu.VMEM((XS, ZS, frame, width), BF16),
            pltpu.VMEM(out_weight.shape, BF16),
            pltpu.VMEM((frame, width), F32),
            pltpu.VMEM((heads, HD, total), BF16),
            pltpu.VMEM((heads, total, frame), F32),
            pltpu.VMEM((heads, total, frame), BF16),
            pltpu.VMEM((heads, HD, total), BF16),
            pltpu.VMEM((heads, HD, frame), F32),
            pltpu.VMEM((heads, total, frame), BF16),
            pltpu.VMEM((2, heads, frame, frame), F32),
            pltpu.VMEM((2, heads, frame, frame), BF16),
            pltpu.VMEM((2, frame, width), F32),
            pltpu.VMEM((2, 3, 8, frame), F32),
            pltpu.VMEM((slots, texts), BF16),
            pltpu.VMEM((2, slots, width), BF16),
            pltpu.VMEM((2, slots // 2, width), BF16),
            pltpu.VMEM((2, slots // 2, width), BF16),
            pltpu.VMEM((2, ys - 1, block, width), BF16),
            pltpu.VMEM((2, block, width), F32),
            pltpu.VMEM((2, reps - 1, CAP, width), F32),
            pltpu.SemaphoreType.REGULAR((2,)),
            dma((7,)),
            dma((2, halves)),
            dma((2, halves)),
            dma((2, 3, halves)),
            dma((2, 3, halves)),
            dma((2, 3)),
            dma((2, 3)),
            dma((6, 2)),
            dma((6, 2)),
            dma((2,)),
            dma((2,)),
            dma((2, ys - 1)),
            dma((2, ys - 1)),
            dma((2, reps - 1)),
            dma((2, reps - 1)),
        ],
        compiler_params=pltpu.CompilerParams(collective_id=0, has_side_effects=True),
    )(
        mask_lists.T,
        text_owner.reshape(1, texts),
        queries,
        keys,
        values,
        grad_output,
        out_weight,
        text_keys,
        text_values,
    )
    return pl.pallas_call(
        hand_over,
        out_shape=shapes,
        in_specs=[pl.BlockSpec(memory_space=pl.ANY)] * 5,
        out_specs=(pl.BlockSpec(memory_space=pl.ANY),) * 5,
        scratch_shapes=[pltpu.VMEM(s.shape, s.dtype) for s in shapes] + [dma((5,)), dma((5,))],
    )(*made)


def solution(mesh):
    rows = P(("seq", "rep"), "head")
    return jax.shard_map(
        functools.partial(local, mesh.shape["seq"], mesh.shape["rep"]),
        mesh=mesh,
        in_specs=(
            rows,
            rows,
            rows,
            rows,
            P("head", None),
            P(None, "head"),
            P(None, "head"),
            P(),
            P(),
        ),
        out_specs=(rows,) * 5,
        check_vma=False,
    )
```

```python
import functools

import jax
import jax.numpy as jnp
from jax import lax
from jax.experimental import pallas as pl
from jax.experimental.pallas import tpu as pltpu
from jax.sharding import PartitionSpec as P

HD = 128
TILE = 128
CAP = 8
XS = 4
ZS = 3
NEG = -1e30
MESH = pl.DeviceIdType.MESH
F32 = jnp.float32
BF16 = jnp.bfloat16


def dot(a, b, contract):
    return lax.dot_general(a, b, (contract, ((), ())), preferred_element_type=F32)


def kernel(
    seqs,
    reps,
    mask_ref,
    owner_ref,
    q_hbm,
    k_hbm,
    v_hbm,
    g_hbm,
    w_hbm,
    tk_hbm,
    tv_hbm,
    dq_ref,
    dk_ref,
    dv_ref,
    tkg_ref,
    tvg_ref,
    qall,
    kall,
    vall,
    gall,
    gbuf,
    w,
    gacc,
    kt,
    st,
    pt,
    vt,
    att,
    ds,
    hp,
    hpt,
    own,
    stat,
    place,
    slots,
    trecv1,
    tsum,
    trecv2,
    t3,
    trecv3,
    ready,
    local_sem,
    zs,
    zr,
    xss,
    xsr,
    xfs,
    xfr,
    hs,
    hr,
    t1s,
    t1r,
    t2s,
    t2r,
    t3s,
    t3r,
):
    seq = lax.axis_index("seq")
    head = lax.axis_index("head")
    rep = lax.axis_index("rep")
    ys = seqs // 2
    y, core = seq // 2, seq % 2
    x, z = head // ZS, head % ZS
    slabs = seqs * reps
    slab = seq * reps + rep
    frame, width = q_hbm.shape
    heads = width // HD
    halves = frame // TILE
    scale = HD ** (-0.5)

    def head_of(dx, dz):
        return ((x + dx + XS) % XS) * ZS + (z + dz + ZS) % ZS

    z_dev = [{"head": head_of(0, 1)}, {"head": head_of(0, -1)}]
    z_of = [(z + 1) % ZS, (z + ZS - 1) % ZS]
    x_dev = [{"head": head_of(1, 0)}, {"head": head_of(-1, 0)}]
    nxt = (slab + 1) % slabs
    prv = (slab + slabs - 1) % slabs
    s_dev = [
        {"seq": nxt // reps, "rep": nxt % reps},
        {"seq": prv // reps, "rep": prv % reps},
    ]
    core_dev = {"seq": y * 2 + 1 - core}
    y_dev = [{"seq": ((y + d) % ys) * 2 + core} for d in range(1, ys)]
    r_dev = [{"rep": (rep + d) % reps} for d in range(1, reps)]

    loads = [
        pltpu.make_async_copy(src, dst, local_sem.at[i])
        for i, (src, dst) in enumerate(
            [
                (q_hbm, qall.at[1]),
                (tk_hbm, kall.at[3]),
                (k_hbm, kall.at[1]),
                (g_hbm, gbuf.at[0, 0]),
                (w_hbm, w),
                (tv_hbm, vall.at[3]),
                (v_hbm, vall.at[1]),
            ]
        )
    ]
    for load in loads:
        load.start()

    for n in range(2):
        stat[n, 1] = jnp.full(stat.shape[2:], NEG, F32)

    barrier = pltpu.get_barrier_semaphore()
    partners = x_dev + s_dev + [core_dev] + y_dev + r_dev
    for dev in partners:
        pl.semaphore_signal(barrier, inc=1, device_id=dev, device_id_type=MESH)
    pl.semaphore_wait(barrier, len(partners) + z)
    for d in range(2):

        @pl.when(z_of[d] > z)
        def _():
            pl.semaphore_signal(barrier, inc=1, device_id=z_dev[d], device_id_type=MESH)

        @pl.when(z_of[d] < z)
        def _():
            pl.semaphore_signal(ready.at[1 - d], inc=1, device_id=z_dev[d], device_id_type=MESH)

    sent = []

    def remote(src, dst, ssem, rsem, dev):
        copy = pltpu.make_async_remote_copy(
            src_ref=src, dst_ref=dst, send_sem=ssem, recv_sem=rsem, device_id=dev, device_id_type=MESH
        )
        sent.append(copy)
        return copy

    def rows(c):
        return pl.ds(c * TILE, TILE)

    def hcols(h):
        return slice(h * HD, (h + 1) * HD)

    hrows = hcols

    zc = [
        [
            remote(g_hbm.at[rows(c)], gbuf.at[0, 1 + d, rows(c)], zs.at[d, c], zr.at[d, c], z_dev[d])
            for c in range(halves)
        ]
        for d in range(2)
    ]
    xc = {}
    xf = {}
    for b in range(3):
        for c in range(halves):
            for d in range(2):
                src = g_hbm.at[rows(c)] if b == 0 else gbuf.at[0, b, rows(c)]
                xc[b, c, d] = remote(
                    src, gbuf.at[1 + d, b, rows(c)], xss.at[d, b, c], xsr.at[d, b, c], x_dev[d]
                )
        for d in range(2):
            xf[b, d] = remote(
                gbuf.at[1 + d, b, rows(d)], gbuf.at[3, b, rows(d)], xfs.at[d, b], xfr.at[d, b], x_dev[d]
            )

    def halo(n, src, dst):
        return [remote(src, dst.at[2 * d], hs.at[n, d], hr.at[n, d], s_dev[d]) for d in range(2)]

    hk = halo(0, k_hbm, kall)
    hv = halo(1, v_hbm, vall)
    hq = halo(2, q_hbm, qall)
    hg = halo(3, gall.at[1], gall)
    ha = halo(4, stat.at[0, 1], stat.at[0])
    hd = halo(5, stat.at[1, 1], stat.at[1])

    def z_send(d):
        for c in range(halves):
            zc[d][c].start()

    def z_send_later(d):
        pl.semaphore_wait(ready.at[d], 1)
        z_send(d)

    for d in range(2):

        @pl.when(z_of[d] < z)
        def _():
            z_send(d)

    for c in range(halves):
        for d in range(2):
            xc[0, c, d].start()
    for copy in hk + hv:
        copy.start()

    lane = lax.broadcasted_iota(jnp.int32, (1, frame), 1)

    def bias_of(tile, of_slab):
        bias = jnp.zeros((1, frame), F32)
        for c in range(halves):
            hit = mask_ref[0, of_slab * halves + c] == tile
            for i in range(1, 3):
                hit = hit | (mask_ref[i, of_slab * halves + c] == tile)
            level = jnp.where(hit, jnp.float32(0.0), jnp.float32(NEG))
            bias = jnp.where(lane // TILE == c, level, bias)
        return bias

    def scores(j):
        for h in range(heads):
            s = dot(kall[j, :, hcols(h)], qall[1, :, hcols(h)], ((1,), (1,))) * scale
            top = stat[0, 1, h : h + 1, :]
            for t in range(halves):
                part = s[t * TILE : (t + 1) * TILE]
                if j < 3:
                    part = part + bias_of((slab - 1 + j) * halves + t, slab)
                st[h, j * frame + t * TILE : j * frame + (t + 1) * TILE, :] = part
                top = jnp.maximum(top, jnp.max(part, axis=0, keepdims=True))
            stat[0, 1, h : h + 1, :] = top

    def transposed_keys(j):
        for h in range(heads):
            kt[h, :, j * frame : (j + 1) * frame] = kall[j, :, hcols(h)].T

    keys_all = st.shape[1]

    def probabilities():
        for d in range(2):
            hk[d].wait_recv()
            scores(2 * d)
        for h in range(heads):
            top = stat[0, 1, h : h + 1, :]
            total = jnp.zeros((1, frame), F32)
            for r in range(0, keys_all, TILE):
                e = jnp.exp(st[h, r : r + TILE, :] - top)
                total = total + jnp.sum(e, axis=0, keepdims=True)
                st[h, r : r + TILE, :] = e
            inv = 1.0 / total
            stat[0, 1, heads + h : heads + h + 1, :] = inv
            for r in range(0, keys_all, TILE):
                p = st[h, r : r + TILE, :] * inv
                st[h, r : r + TILE, :] = p
                pt[h, r : r + TILE, :] = p.astype(BF16)
        for d in range(2):
            ha[d].start()
            transposed_keys(2 * d)

    loads[0].wait()
    loads[1].wait()
    scores(3)
    loads[2].wait()
    scores(1)

    def forward(b):
        for d in range(2):
            xc[b, d, d].wait_recv()
            xf[b, d].start()

    def add_block(c, xslot, b):
        hd_at = head_of((0, -1, 1, 2)[xslot], (0, -1, 1)[b])
        cols = pl.ds(pl.multiple_of(hd_at * frame, frame), frame)
        gacc[:, c * TILE : (c + 1) * TILE] += dot(w[:, cols], gbuf[xslot, b, rows(c), :], ((1,), (1,)))

    forward(0)
    loads[3].wait()
    loads[4].wait()
    gacc[...] = jnp.zeros_like(gacc)
    for c in range(halves):
        add_block(c, 0, 0)

    owner = owner_ref[...]
    texts = owner.shape[1]
    row_i = lax.broadcasted_iota(jnp.int32, (texts, texts), 0)
    col_i = lax.broadcasted_iota(jnp.int32, (texts, texts), 1)
    owner_f = owner.astype(F32)
    owner_col = jnp.sum(jnp.where(row_i == col_i, owner_f, 0.0), axis=1, keepdims=True)
    same = (owner_col == owner_f) & (row_i < col_i)
    rank = jnp.sum(jnp.where(same, 1.0, 0.0), axis=0, keepdims=True).astype(jnp.int32)
    o_rep = owner % reps
    o_seq = owner // reps
    where_to = (((o_seq % 2) * ys + o_seq // 2) * reps + o_rep) * CAP + rank
    slot_i = lax.broadcasted_iota(jnp.int32, place.shape, 0)
    place[...] = jnp.where(slot_i == where_to, 1.0, 0.0).astype(BF16)
    transposed_keys(3)
    transposed_keys(1)

    @pl.when(z == 0)
    def _():
        z_send_later(0)
        probabilities()
        z_send_later(1)

    @pl.when(z == 1)
    def _():
        z_send_later(0)

    @pl.when(z < 2)
    def _():
        for copy in hq:
            copy.start()

    @pl.when(z == 1)
    def _():
        probabilities()

    for d in range(2):
        xc[0, 1 - d, d].wait_recv()
    for e in range(1, 3):
        for c in range(halves):
            add_block(c, e, 0)
    for c in range(halves):
        xf[0, c].wait_recv()
        add_block(c, 3, 0)
    for c in range(halves):
        for d in range(2):
            zc[d][c].wait_recv()
            for e in range(2):
                xc[1 + d, c, e].start()
    @pl.when(z == 2)
    def _():
        for copy in hq:
            copy.start()
        probabilities()

    for b in range(1, 3):
        forward(b)
    for c in range(halves):
        for b in range(1, 3):
            add_block(c, 0, b)
    loads[5].wait()
    loads[6].wait()
    for d in range(2):
        hv[d].wait_recv()
    for h in range(heads):
        for j in range(4):
            vt[h, :, j * frame : (j + 1) * frame] = vall[j, :, hcols(h)].T
        att[h] = dot(vt[h], pt[h], ((1,), (0,)))
    for b in range(1, 3):
        for d in range(2):
            xc[b, 1 - d, d].wait_recv()
            for c in range(halves):
                add_block(c, 1 + d, b)
    for b in range(1, 3):
        for c in range(halves):
            xf[b, c].wait_recv()
            add_block(c, 3, b)
    gall[1] = gacc[...].astype(BF16)
    for copy in hg:
        copy.start()

    def value_part(j, h):
        return dot(pt[h, j * frame : (j + 1) * frame, :], gall[1, hrows(h), :], ((1,), (1,)))

    def key_part(j, h):
        return dot(ds[h, j * frame : (j + 1) * frame, :], qall[1, :, hcols(h)], ((1,), (0,)))

    half = slots.shape[1] // 2
    block = reps * CAP
    first = [
        remote(slots.at[n, pl.ds((1 - core) * half, half)], trecv1.at[n], t1s.at[n], t1r.at[n], core_dev)
        for n in range(2)
    ]
    second = [
        [
            remote(
                tsum.at[n, pl.ds(((y + d) % ys) * block, block)],
                trecv2.at[n, d - 1],
                t2s.at[n, d - 1],
                t2r.at[n, d - 1],
                y_dev[d - 1],
            )
            for d in range(1, ys)
        ]
        for n in range(2)
    ]
    third = [
        [
            remote(
                t3.at[n, pl.ds(((rep + d) % reps) * CAP, CAP)],
                trecv3.at[n, d - 1],
                t3s.at[n, d - 1],
                t3r.at[n, d - 1],
                r_dev[d - 1],
            )
            for d in range(1, reps)
        ]
        for n in range(2)
    ]

    def text_first(n, part):
        for h in range(heads):
            placed = dot(place[...], part(3, h).astype(BF16), ((1,), (0,)))
            slots[n, :, hcols(h)] = placed.astype(BF16)
        first[n].start()

    def text_second(n):
        first[n].wait_recv()
        mine = slots[n, pl.ds(core * half, half), :].astype(F32)
        tsum[n] = (mine + trecv1[n].astype(F32)).astype(BF16)
        for d in sorted(range(1, ys), key=lambda d: -min(d, ys - d)):
            second[n][d - 1].start()

    def text_third(n):
        total = tsum[n, pl.ds(y * block, block), :].astype(F32)
        for d in range(1, ys):
            second[n][d - 1].wait_recv()
            total = total + trecv2[n, d - 1].astype(F32)
        t3[n] = total
        for copy in third[n]:
            copy.start()

    def text_last(n, out):
        total = t3[n, pl.ds(rep * CAP, CAP), :]
        for d in range(1, reps):
            third[n][d - 1].wait_recv()
            total = total + trecv3[n, d - 1]
        out[...] = total.astype(BF16)

    delta = []
    for h in range(heads):
        delta.append(jnp.sum(gall[1, hrows(h), :].astype(F32) * att[h], axis=0, keepdims=True))
        stat[1, 1, h : h + 1, :] = delta[h]
    for copy in hd:
        copy.start()

    def dscore(j):
        for h in range(heads):
            for t in range(halves):
                r = j * frame + t * TILE
                part = dot(vall[j, rows(t), hcols(h)], gall[1, hrows(h), :], ((1,), (0,)))
                ds[h, r : r + TILE, :] = (st[h, r : r + TILE, :] * (part - delta[h])).astype(BF16)

    text_first(0, value_part)
    dscore(3)
    text_first(1, lambda j, h: key_part(j, h) * scale)
    text_second(0)
    dscore(1)
    text_second(1)
    for h in range(heads):
        own[0, :, hcols(h)] = value_part(1, h)
    dscore(0)
    dscore(2)
    for h in range(heads):
        own[1, :, hcols(h)] = key_part(1, h)
    for h in range(heads):
        dqt = dot(kt[h], ds[h], ((1,), (0,))) * scale
        dq_ref[:, hcols(h)] = dqt.T.astype(BF16)
    text_third(0)

    for d in range(2):
        hq[d].wait_recv()
        ha[d].wait_recv()
        for h in range(heads):
            s = dot(kall[1, :, hcols(h)], qall[2 * d, :, hcols(h)], ((1,), (1,))) * scale
            top = stat[0, 2 * d, h : h + 1, :]
            inv = stat[0, 2 * d, heads + h : heads + h + 1, :]
            for t in range(halves):
                part = s[t * TILE : (t + 1) * TILE] + bias_of(slab * halves + t, (prv, nxt)[d])
                p = jnp.exp(part - top) * inv
                hp[d, h, rows(t), :] = p
                hpt[d, h, rows(t), :] = p.astype(BF16)
    text_third(1)
    for d in range(2):
        hd[d].wait_recv()
        hg[d].wait_recv()
        for h in range(heads):
            g = gall[2 * d, hrows(h), :]
            own[0, :, hcols(h)] += dot(hpt[d, h], g, ((1,), (1,)))
            dph = dot(vall[1, :, hcols(h)], g, ((1,), (0,)))
            dsh = (hp[d, h] * (dph - stat[1, 2 * d, h : h + 1, :])).astype(BF16)
            own[1, :, hcols(h)] += dot(dsh, qall[2 * d, :, hcols(h)], ((1,), (0,)))
    dv_ref[...] = own[0].astype(BF16)
    dk_ref[...] = (own[1] * scale).astype(BF16)
    text_last(0, tvg_ref)
    text_last(1, tkg_ref)

    for copy in sent:
        copy.wait_send()


def hand_over(*refs):
    count = (len(refs) - 2) // 3
    given, taken, held = refs[:count], refs[count : 2 * count], refs[2 * count : 3 * count]
    in_sem, out_sem = refs[3 * count :]
    ins = [pltpu.make_async_copy(given[i], held[i], in_sem.at[i]) for i in range(count)]
    outs = [pltpu.make_async_copy(held[i], taken[i], out_sem.at[i]) for i in range(count)]
    for copy in ins:
        copy.start()
    for i in range(count):
        ins[i].wait()
        outs[i].start()
    for copy in outs:
        copy.wait()


def local(
    seqs,
    reps,
    queries,
    keys,
    values,
    grad_output,
    out_weight,
    text_keys,
    text_values,
    mask_lists,
    text_owner,
):
    frame, width = queries.shape
    texts = text_keys.shape[0]
    heads = width // HD
    ys = seqs // 2
    slots = seqs * reps * CAP
    halves = frame // TILE
    block = reps * CAP
    total = 3 * frame + texts
    grads = jax.ShapeDtypeStruct((frame, width), BF16)
    text_grads = jax.ShapeDtypeStruct((CAP, width), BF16)
    hbm = pl.BlockSpec(memory_space=pltpu.HBM)
    vmem = pl.BlockSpec(memory_space=pltpu.VMEM)
    dma = pltpu.SemaphoreType.DMA
    shapes = (grads, grads, grads, text_grads, text_grads)
    made = pl.pallas_call(
        functools.partial(kernel, seqs, reps),
        out_shape=shapes,
        in_specs=[pl.BlockSpec(memory_space=pltpu.SMEM), vmem] + [hbm] * 7,
        out_specs=(vmem,) * 5,
        scratch_shapes=[
            pltpu.VMEM((3, frame, width), BF16),
            pltpu.VMEM((4, frame, width), BF16),
            pltpu.VMEM((4, frame, width), BF16),
            pltpu.VMEM((3, frame, width), BF16),
            pltpu.VMEM((XS, ZS, frame, width), BF16),
            pltpu.VMEM(out_weight.shape, BF16),
            pltpu.VMEM((frame, width), F32),
            pltpu.VMEM((heads, HD, total), BF16),
            pltpu.VMEM((heads, total, frame), F32),
            pltpu.VMEM((heads, total, frame), BF16),
            pltpu.VMEM((heads, HD, total), BF16),
            pltpu.VMEM((heads, HD, frame), F32),
            pltpu.VMEM((heads, total, frame), BF16),
            pltpu.VMEM((2, heads, frame, frame), F32),
            pltpu.VMEM((2, heads, frame, frame), BF16),
            pltpu.VMEM((2, frame, width), F32),
            pltpu.VMEM((2, 3, 8, frame), F32),
            pltpu.VMEM((slots, texts), BF16),
            pltpu.VMEM((2, slots, width), BF16),
            pltpu.VMEM((2, slots // 2, width), BF16),
            pltpu.VMEM((2, slots // 2, width), BF16),
            pltpu.VMEM((2, ys - 1, block, width), BF16),
            pltpu.VMEM((2, block, width), F32),
            pltpu.VMEM((2, reps - 1, CAP, width), F32),
            pltpu.SemaphoreType.REGULAR((2,)),
            dma((7,)),
            dma((2, halves)),
            dma((2, halves)),
            dma((2, 3, halves)),
            dma((2, 3, halves)),
            dma((2, 3)),
            dma((2, 3)),
            dma((6, 2)),
            dma((6, 2)),
            dma((2,)),
            dma((2,)),
            dma((2, ys - 1)),
            dma((2, ys - 1)),
            dma((2, reps - 1)),
            dma((2, reps - 1)),
        ],
        compiler_params=pltpu.CompilerParams(collective_id=0, has_side_effects=True),
    )(
        mask_lists.T,
        text_owner.reshape(1, texts),
        queries,
        keys,
        values,
        grad_output,
        out_weight,
        text_keys,
        text_values,
    )
    return pl.pallas_call(
        hand_over,
        out_shape=shapes,
        in_specs=[pl.BlockSpec(memory_space=pl.ANY)] * 5,
        out_specs=(pl.BlockSpec(memory_space=pl.ANY),) * 5,
        scratch_shapes=[pltpu.VMEM(s.shape, s.dtype) for s in shapes] + [dma((5,)), dma((5,))],
    )(*made)


def solution(mesh):
    rows = P(("seq", "rep"), "head")
    return jax.shard_map(
        functools.partial(local, mesh.shape["seq"], mesh.shape["rep"]),
        mesh=mesh,
        in_specs=(
            rows,
            rows,
            rows,
            rows,
            P("head", None),
            P(None, "head"),
            P(None, "head"),
            P(),
            P(),
        ),
        out_specs=(rows,) * 5,
        check_vma=False,
    )
```

```python
import functools

import jax
import jax.numpy as jnp
from jax import lax
from jax.experimental import pallas as pl
from jax.experimental.pallas import tpu as pltpu
from jax.sharding import PartitionSpec as P

HD = 128
TILE = 128
CAP = 8
XS = 4
ZS = 3
NEG = -1e30
MESH = pl.DeviceIdType.MESH
F32 = jnp.float32
BF16 = jnp.bfloat16


def dot(a, b, contract):
    return lax.dot_general(a, b, (contract, ((), ())), preferred_element_type=F32)


def kernel(
    seqs,
    reps,
    mask_ref,
    owner_ref,
    q_hbm,
    k_hbm,
    v_hbm,
    g_hbm,
    w_hbm,
    tk_hbm,
    tv_hbm,
    dq_ref,
    dk_ref,
    dv_ref,
    tkg_ref,
    tvg_ref,
    qall,
    kall,
    vall,
    gall,
    gbuf,
    w,
    gacc,
    kt,
    st,
    pt,
    vt,
    att,
    ds,
    hp,
    hpt,
    own,
    stat,
    place,
    slots,
    trecv1,
    tsum,
    trecv2,
    t3,
    trecv3,
    ready,
    local_sem,
    zs,
    zr,
    xss,
    xsr,
    xfs,
    xfr,
    hs,
    hr,
    t1s,
    t1r,
    t2s,
    t2r,
    t3s,
    t3r,
):
    seq = lax.axis_index("seq")
    head = lax.axis_index("head")
    rep = lax.axis_index("rep")
    ys = seqs // 2
    y, core = seq // 2, seq % 2
    x, z = head // ZS, head % ZS
    slabs = seqs * reps
    slab = seq * reps + rep
    frame, width = q_hbm.shape
    heads = width // HD
    halves = frame // TILE
    scale = HD ** (-0.5)

    def head_of(dx, dz):
        return ((x + dx + XS) % XS) * ZS + (z + dz + ZS) % ZS

    z_dev = [{"head": head_of(0, 1)}, {"head": head_of(0, -1)}]
    z_of = [(z + 1) % ZS, (z + ZS - 1) % ZS]
    x_dev = [{"head": head_of(1, 0)}, {"head": head_of(-1, 0)}]
    nxt = (slab + 1) % slabs
    prv = (slab + slabs - 1) % slabs
    s_dev = [
        {"seq": nxt // reps, "rep": nxt % reps},
        {"seq": prv // reps, "rep": prv % reps},
    ]
    core_dev = {"seq": y * 2 + 1 - core}
    y_dev = [{"seq": ((y + d) % ys) * 2 + core} for d in range(1, ys)]
    r_dev = [{"rep": (rep + d) % reps} for d in range(1, reps)]

    loads = [
        pltpu.make_async_copy(src, dst, local_sem.at[i])
        for i, (src, dst) in enumerate(
            [
                (q_hbm, qall.at[1]),
                (tk_hbm, kall.at[3]),
                (k_hbm, kall.at[1]),
                (g_hbm, gbuf.at[0, 0]),
                (w_hbm, w),
                (tv_hbm, vall.at[3]),
                (v_hbm, vall.at[1]),
            ]
        )
    ]
    for load in loads:
        load.start()

    for n in range(2):
        stat[n, 1] = jnp.full(stat.shape[2:], NEG, F32)

    barrier = pltpu.get_barrier_semaphore()
    partners = x_dev + s_dev + [core_dev] + y_dev + r_dev
    for dev in partners:
        pl.semaphore_signal(barrier, inc=1, device_id=dev, device_id_type=MESH)
    pl.semaphore_wait(barrier, len(partners) + z)
    for d in range(2):

        @pl.when(z_of[d] > z)
        def _():
            pl.semaphore_signal(barrier, inc=1, device_id=z_dev[d], device_id_type=MESH)

        @pl.when(z_of[d] < z)
        def _():
            pl.semaphore_signal(ready.at[1 - d], inc=1, device_id=z_dev[d], device_id_type=MESH)

    sent = []

    def remote(src, dst, ssem, rsem, dev):
        copy = pltpu.make_async_remote_copy(
            src_ref=src, dst_ref=dst, send_sem=ssem, recv_sem=rsem, device_id=dev, device_id_type=MESH
        )
        sent.append(copy)
        return copy

    def rows(c):
        return pl.ds(c * TILE, TILE)

    def hcols(h):
        return slice(h * HD, (h + 1) * HD)

    hrows = hcols

    zc = [
        [
            remote(g_hbm.at[rows(c)], gbuf.at[0, 1 + d, rows(c)], zs.at[d, c], zr.at[d, c], z_dev[d])
            for c in range(halves)
        ]
        for d in range(2)
    ]
    xc = {}
    xf = {}
    for b in range(3):
        for c in range(halves):
            for d in range(2):
                src = g_hbm.at[rows(c)] if b == 0 else gbuf.at[0, b, rows(c)]
                xc[b, c, d] = remote(
                    src, gbuf.at[1 + d, b, rows(c)], xss.at[d, b, c], xsr.at[d, b, c], x_dev[d]
                )
        for d in range(2):
            xf[b, d] = remote(
                gbuf.at[1 + d, b, rows(d)], gbuf.at[3, b, rows(d)], xfs.at[d, b], xfr.at[d, b], x_dev[d]
            )

    def halo(n, src, dst):
        return [remote(src, dst.at[2 * d], hs.at[n, d], hr.at[n, d], s_dev[d]) for d in range(2)]

    hk = halo(0, k_hbm, kall)
    hv = halo(1, v_hbm, vall)
    hq = halo(2, q_hbm, qall)
    hg = halo(3, gall.at[1], gall)
    ha = halo(4, stat.at[0, 1], stat.at[0])
    hd = halo(5, stat.at[1, 1], stat.at[1])

    def z_send(d):
        for c in range(halves):
            zc[d][c].start()

    def z_send_later(d):
        pl.semaphore_wait(ready.at[d], 1)
        z_send(d)

    for d in range(2):

        @pl.when(z_of[d] < z)
        def _():
            z_send(d)

    for c in range(halves):
        for d in range(2):
            xc[0, c, d].start()
    for copy in hk + hv:
        copy.start()

    lane = lax.broadcasted_iota(jnp.int32, (1, frame), 1)

    def bias_of(tile, of_slab):
        bias = jnp.zeros((1, frame), F32)
        for c in range(halves):
            hit = mask_ref[0, of_slab * halves + c] == tile
            for i in range(1, 3):
                hit = hit | (mask_ref[i, of_slab * halves + c] == tile)
            level = jnp.where(hit, jnp.float32(0.0), jnp.float32(NEG))
            bias = jnp.where(lane // TILE == c, level, bias)
        return bias

    def scores(j):
        for h in range(heads):
            s = dot(kall[j, :, hcols(h)], qall[1, :, hcols(h)], ((1,), (1,))) * scale
            top = stat[0, 1, h : h + 1, :]
            for t in range(halves):
                part = s[t * TILE : (t + 1) * TILE]
                if j < 3:
                    part = part + bias_of((slab - 1 + j) * halves + t, slab)
                st[h, j * frame + t * TILE : j * frame + (t + 1) * TILE, :] = part
                top = jnp.maximum(top, jnp.max(part, axis=0, keepdims=True))
            stat[0, 1, h : h + 1, :] = top

    def transposed_keys(j):
        for h in range(heads):
            kt[h, :, j * frame : (j + 1) * frame] = kall[j, :, hcols(h)].T

    keys_all = st.shape[1]

    def probabilities():
        for d in range(2):
            hk[d].wait_recv()
            scores(2 * d)
        for h in range(heads):
            top = stat[0, 1, h : h + 1, :]
            total = jnp.zeros((1, frame), F32)
            for r in range(0, keys_all, TILE):
                e = jnp.exp(st[h, r : r + TILE, :] - top)
                total = total + jnp.sum(e, axis=0, keepdims=True)
                st[h, r : r + TILE, :] = e
            inv = 1.0 / total
            stat[0, 1, heads + h : heads + h + 1, :] = inv
            for r in range(0, keys_all, TILE):
                p = st[h, r : r + TILE, :] * inv
                st[h, r : r + TILE, :] = p
                pt[h, r : r + TILE, :] = p.astype(BF16)
        for d in range(2):
            ha[d].start()
            transposed_keys(2 * d)

    loads[0].wait()
    loads[1].wait()
    scores(3)
    loads[2].wait()
    scores(1)

    def forward(b):
        for d in range(2):
            xc[b, d, d].wait_recv()
            xf[b, d].start()

    def add_block(c, xslot, b):
        hd_at = head_of((0, -1, 1, 2)[xslot], (0, -1, 1)[b])
        cols = pl.ds(pl.multiple_of(hd_at * frame, frame), frame)
        gacc[:, c * TILE : (c + 1) * TILE] += dot(w[:, cols], gbuf[xslot, b, rows(c), :], ((1,), (1,)))

    forward(0)
    loads[3].wait()
    loads[4].wait()
    gacc[...] = jnp.zeros_like(gacc)
    for c in range(halves):
        add_block(c, 0, 0)

    owner = owner_ref[...]
    texts = owner.shape[1]
    row_i = lax.broadcasted_iota(jnp.int32, (texts, texts), 0)
    col_i = lax.broadcasted_iota(jnp.int32, (texts, texts), 1)
    owner_f = owner.astype(F32)
    owner_col = jnp.sum(jnp.where(row_i == col_i, owner_f, 0.0), axis=1, keepdims=True)
    same = (owner_col == owner_f) & (row_i < col_i)
    rank = jnp.sum(jnp.where(same, 1.0, 0.0), axis=0, keepdims=True).astype(jnp.int32)
    o_rep = owner % reps
    o_seq = owner // reps
    where_to = (((o_seq % 2) * ys + o_seq // 2) * reps + o_rep) * CAP + rank
    slot_i = lax.broadcasted_iota(jnp.int32, place.shape, 0)
    place[...] = jnp.where(slot_i == where_to, 1.0, 0.0).astype(BF16)
    transposed_keys(3)
    transposed_keys(1)

    @pl.when(z == 0)
    def _():
        z_send_later(0)
        probabilities()
        z_send_later(1)

    @pl.when(z == 1)
    def _():
        z_send_later(0)

    for copy in hq:
        copy.start()

    @pl.when(z == 1)
    def _():
        probabilities()

    for d in range(2):
        xc[0, 1 - d, d].wait_recv()
    for e in range(1, 3):
        for c in range(halves):
            add_block(c, e, 0)
    for c in range(halves):
        xf[0, c].wait_recv()
        add_block(c, 3, 0)
    for c in range(halves):
        for d in range(2):
            zc[d][c].wait_recv()
            for e in range(2):
                xc[1 + d, c, e].start()
    @pl.when(z == 2)
    def _():
        probabilities()

    for b in range(1, 3):
        forward(b)
    for c in range(halves):
        for b in range(1, 3):
            add_block(c, 0, b)
    def attend():
        loads[5].wait()
        loads[6].wait()
        for d in range(2):
            hv[d].wait_recv()
        for h in range(heads):
            for j in range(4):
                vt[h, :, j * frame : (j + 1) * frame] = vall[j, :, hcols(h)].T
            att[h] = dot(vt[h], pt[h], ((1,), (0,)))

    @pl.when(z < 2)
    def _():
        attend()

    for b in range(1, 3):
        for d in range(2):
            xc[b, 1 - d, d].wait_recv()
            for c in range(halves):
                add_block(c, 1 + d, b)
    for b in range(1, 3):
        for c in range(halves):
            xf[b, c].wait_recv()
            add_block(c, 3, b)
    gall[1] = gacc[...].astype(BF16)
    for copy in hg:
        copy.start()

    def value_part(j, h):
        return dot(pt[h, j * frame : (j + 1) * frame, :], gall[1, hrows(h), :], ((1,), (1,)))

    def key_part(j, h):
        return dot(ds[h, j * frame : (j + 1) * frame, :], qall[1, :, hcols(h)], ((1,), (0,)))

    half = slots.shape[1] // 2
    block = reps * CAP
    first = [
        remote(slots.at[n, pl.ds((1 - core) * half, half)], trecv1.at[n], t1s.at[n], t1r.at[n], core_dev)
        for n in range(2)
    ]
    second = [
        [
            remote(
                tsum.at[n, pl.ds(((y + d) % ys) * block, block)],
                trecv2.at[n, d - 1],
                t2s.at[n, d - 1],
                t2r.at[n, d - 1],
                y_dev[d - 1],
            )
            for d in range(1, ys)
        ]
        for n in range(2)
    ]
    third = [
        [
            remote(
                t3.at[n, pl.ds(((rep + d) % reps) * CAP, CAP)],
                trecv3.at[n, d - 1],
                t3s.at[n, d - 1],
                t3r.at[n, d - 1],
                r_dev[d - 1],
            )
            for d in range(1, reps)
        ]
        for n in range(2)
    ]

    def text_first(n, part):
        for h in range(heads):
            placed = dot(place[...], part(3, h).astype(BF16), ((1,), (0,)))
            slots[n, :, hcols(h)] = placed.astype(BF16)
        first[n].start()

    def text_second(n):
        first[n].wait_recv()
        mine = slots[n, pl.ds(core * half, half), :].astype(F32)
        tsum[n] = (mine + trecv1[n].astype(F32)).astype(BF16)
        for d in sorted(range(1, ys), key=lambda d: -min(d, ys - d)):
            second[n][d - 1].start()

    def text_third(n):
        total = tsum[n, pl.ds(y * block, block), :].astype(F32)
        for d in range(1, ys):
            second[n][d - 1].wait_recv()
            total = total + trecv2[n, d - 1].astype(F32)
        t3[n] = total
        for copy in third[n]:
            copy.start()

    def text_last(n, out):
        total = t3[n, pl.ds(rep * CAP, CAP), :]
        for d in range(1, reps):
            third[n][d - 1].wait_recv()
            total = total + trecv3[n, d - 1]
        out[...] = total.astype(BF16)

    def dscore(j):
        for h in range(heads):
            for t in range(halves):
                r = j * frame + t * TILE
                part = dot(vall[j, rows(t), hcols(h)], gall[1, hrows(h), :], ((1,), (0,)))
                ds[h, r : r + TILE, :] = (st[h, r : r + TILE, :] * (part - delta[h])).astype(BF16)

    text_first(0, value_part)

    @pl.when(z == 2)
    def _():
        attend()

    delta = []
    for h in range(heads):
        delta.append(jnp.sum(gall[1, hrows(h), :].astype(F32) * att[h], axis=0, keepdims=True))
        stat[1, 1, h : h + 1, :] = delta[h]
    for copy in hd:
        copy.start()

    dscore(3)
    text_first(1, lambda j, h: key_part(j, h) * scale)
    text_second(0)
    dscore(1)
    text_second(1)
    for h in range(heads):
        own[0, :, hcols(h)] = value_part(1, h)
    dscore(0)
    dscore(2)
    for h in range(heads):
        own[1, :, hcols(h)] = key_part(1, h)
    for h in range(heads):
        dqt = dot(kt[h], ds[h], ((1,), (0,))) * scale
        dq_ref[:, hcols(h)] = dqt.T.astype(BF16)
    text_third(0)

    for d in range(2):
        hq[d].wait_recv()
        ha[d].wait_recv()
        for h in range(heads):
            s = dot(kall[1, :, hcols(h)], qall[2 * d, :, hcols(h)], ((1,), (1,))) * scale
            top = stat[0, 2 * d, h : h + 1, :]
            inv = stat[0, 2 * d, heads + h : heads + h + 1, :]
            for t in range(halves):
                part = s[t * TILE : (t + 1) * TILE] + bias_of(slab * halves + t, (prv, nxt)[d])
                p = jnp.exp(part - top) * inv
                hp[d, h, rows(t), :] = p
                hpt[d, h, rows(t), :] = p.astype(BF16)
    text_third(1)
    for d in range(2):
        hd[d].wait_recv()
        hg[d].wait_recv()
        for h in range(heads):
            g = gall[2 * d, hrows(h), :]
            own[0, :, hcols(h)] += dot(hpt[d, h], g, ((1,), (1,)))
            dph = dot(vall[1, :, hcols(h)], g, ((1,), (0,)))
            dsh = (hp[d, h] * (dph - stat[1, 2 * d, h : h + 1, :])).astype(BF16)
            own[1, :, hcols(h)] += dot(dsh, qall[2 * d, :, hcols(h)], ((1,), (0,)))
    dv_ref[...] = own[0].astype(BF16)
    dk_ref[...] = (own[1] * scale).astype(BF16)
    text_last(0, tvg_ref)
    text_last(1, tkg_ref)

    for copy in sent:
        copy.wait_send()


def hand_over(*refs):
    count = (len(refs) - 2) // 3
    given, taken, held = refs[:count], refs[count : 2 * count], refs[2 * count : 3 * count]
    in_sem, out_sem = refs[3 * count :]
    ins = [pltpu.make_async_copy(given[i], held[i], in_sem.at[i]) for i in range(count)]
    outs = [pltpu.make_async_copy(held[i], taken[i], out_sem.at[i]) for i in range(count)]
    for copy in ins:
        copy.start()
    for i in range(count):
        ins[i].wait()
        outs[i].start()
    for copy in outs:
        copy.wait()


def local(
    seqs,
    reps,
    queries,
    keys,
    values,
    grad_output,
    out_weight,
    text_keys,
    text_values,
    mask_lists,
    text_owner,
):
    frame, width = queries.shape
    texts = text_keys.shape[0]
    heads = width // HD
    ys = seqs // 2
    slots = seqs * reps * CAP
    halves = frame // TILE
    block = reps * CAP
    total = 3 * frame + texts
    grads = jax.ShapeDtypeStruct((frame, width), BF16)
    text_grads = jax.ShapeDtypeStruct((CAP, width), BF16)
    hbm = pl.BlockSpec(memory_space=pltpu.HBM)
    vmem = pl.BlockSpec(memory_space=pltpu.VMEM)
    dma = pltpu.SemaphoreType.DMA
    shapes = (grads, grads, grads, text_grads, text_grads)
    made = pl.pallas_call(
        functools.partial(kernel, seqs, reps),
        out_shape=shapes,
        in_specs=[pl.BlockSpec(memory_space=pltpu.SMEM), vmem] + [hbm] * 7,
        out_specs=(vmem,) * 5,
        scratch_shapes=[
            pltpu.VMEM((3, frame, width), BF16),
            pltpu.VMEM((4, frame, width), BF16),
            pltpu.VMEM((4, frame, width), BF16),
            pltpu.VMEM((3, frame, width), BF16),
            pltpu.VMEM((XS, ZS, frame, width), BF16),
            pltpu.VMEM(out_weight.shape, BF16),
            pltpu.VMEM((frame, width), F32),
            pltpu.VMEM((heads, HD, total), BF16),
            pltpu.VMEM((heads, total, frame), F32),
            pltpu.VMEM((heads, total, frame), BF16),
            pltpu.VMEM((heads, HD, total), BF16),
            pltpu.VMEM((heads, HD, frame), F32),
            pltpu.VMEM((heads, total, frame), BF16),
            pltpu.VMEM((2, heads, frame, frame), F32),
            pltpu.VMEM((2, heads, frame, frame), BF16),
            pltpu.VMEM((2, frame, width), F32),
            pltpu.VMEM((2, 3, 8, frame), F32),
            pltpu.VMEM((slots, texts), BF16),
            pltpu.VMEM((2, slots, width), BF16),
            pltpu.VMEM((2, slots // 2, width), BF16),
            pltpu.VMEM((2, slots // 2, width), BF16),
            pltpu.VMEM((2, ys - 1, block, width), BF16),
            pltpu.VMEM((2, block, width), F32),
            pltpu.VMEM((2, reps - 1, CAP, width), F32),
            pltpu.SemaphoreType.REGULAR((2,)),
            dma((7,)),
            dma((2, halves)),
            dma((2, halves)),
            dma((2, 3, halves)),
            dma((2, 3, halves)),
            dma((2, 3)),
            dma((2, 3)),
            dma((6, 2)),
            dma((6, 2)),
            dma((2,)),
            dma((2,)),
            dma((2, ys - 1)),
            dma((2, ys - 1)),
            dma((2, reps - 1)),
            dma((2, reps - 1)),
        ],
        compiler_params=pltpu.CompilerParams(collective_id=0, has_side_effects=True),
    )(
        mask_lists.T,
        text_owner.reshape(1, texts),
        queries,
        keys,
        values,
        grad_output,
        out_weight,
        text_keys,
        text_values,
    )
    return pl.pallas_call(
        hand_over,
        out_shape=shapes,
        in_specs=[pl.BlockSpec(memory_space=pl.ANY)] * 5,
        out_specs=(pl.BlockSpec(memory_space=pl.ANY),) * 5,
        scratch_shapes=[pltpu.VMEM(s.shape, s.dtype) for s in shapes] + [dma((5,)), dma((5,))],
    )(*made)


def solution(mesh):
    rows = P(("seq", "rep"), "head")
    return jax.shard_map(
        functools.partial(local, mesh.shape["seq"], mesh.shape["rep"]),
        mesh=mesh,
        in_specs=(
            rows,
            rows,
            rows,
            rows,
            P("head", None),
            P(None, "head"),
            P(None, "head"),
            P(),
            P(),
        ),
        out_specs=(rows,) * 5,
        check_vma=False,
    )
```
